32 devices in a mesh: cuts: 2 (over y), qa: 16 (over z, x, core).
Axes of the slice: x: 2, y: 2, z: 4, core: 2. Of those that a mesh axis runs over, the one named last changes fastest.
Arguments:
- state: float32 [2, 4194304], P(None, ('cuts', 'qa')), parts along dimension 1, may hold values from -6 to 6
- unitaries: float32 [12, 2, 128, 128], replicated, may hold values from -1 to 1, as said below
- gate_order: int32 [12], replicated, may hold values from 0 to 11, each once
- gate_starts: int32 [12], replicated, may hold values from 0 to 1
- pair_gates: float32 [2, 2, 2, 2], replicated, may hold values from -1 to 1, as said below
Outputs:
- final_state: float32 [2, 4194304], P(None, ('cuts', 'qa')), parts along dimension 1
The draws below stay inside these ranges and needn't reach their ends.
There are 2 independent parts, one for each index of `cuts`. The reference program is written for one: setup_inputs(seed, part) draws one part's arguments, and reference() takes and returns one part's arrays. A program takes and returns all parts, laid end to end along the dimension named above; an argument that names none is the same for every part. Nothing has to cross between parts.
Inputs may be any that keep to these rules, and one draw needn't show every extreme that they name: For every k, unitaries[k, 0] + i unitaries[k, 1] is a unitary matrix. For each p, pair_gates[p, 0] + i pair_gates[p, 1] is a unitary 2 x 2 matrix. `gate_order`: A permutation of 0 .. 11.
All inputs are finite; a program needn't handle non-finite values.
Results may differ from the reference program's by a relative error of at most 0.0003.
Values sent between devices are 32-bit elements; how exact they have to be, the bound alone decides.
No kernel may reach another device: no remote copies, remote signals or barrier semaphores. Data moves between devices by JAX's collectives and lax.ppermute only.
A program may use at most 64 MiB of HBM per device.

```python
from functools import partial
import jax
import jax.numpy as jnp
from jax import lax

AMP_DEV = 131072
GDIM = 128
NGATES = 12
QA_DEVS = 16
AMPS = 2097152


def unitary_batch(key, count, dim):
    key_re, key_im = jax.random.split(jax.random.fold_in(key, 17))
    part_re = jax.random.normal(key_re, (count, dim, dim), jnp.float32)
    part_im = jax.random.normal(key_im, (count, dim, dim), jnp.float32)
    upper = jnp.concatenate([part_re, -part_im], axis=2)
    lower = jnp.concatenate([part_im, part_re], axis=2)
    embedded = jnp.concatenate([upper, lower], axis=1)
    left, values, right = jnp.linalg.svd(embedded)
    polar = jnp.matmul(left, right, precision=lax.Precision.HIGHEST)
    return jnp.stack([polar[:, :dim, :dim], polar[:, dim:, :dim]], axis=1)


def draw_unitaries(key, part):
    return unitary_batch(key, NGATES, GDIM).astype(jnp.float32)


def draw_pair_gates(key, part):
    return unitary_batch(jax.random.fold_in(key, 5), 2, 2).astype(jnp.float32)


def place_ends(drawn, rng, least, top_value):
    extent = drawn.shape
    index_at = [jax.random.randint(jax.random.fold_in(rng, axis), (), 0, extent[axis]) for axis in range(len(extent))]
    drawn = drawn.at[tuple(index_at)].set(least)
    longest = extent.index(max(extent))
    index_at[longest] = (index_at[longest] + 1) % extent[longest]
    return drawn.at[tuple(index_at)].set(top_value)


def steps_of(stream_key, dims, pieces, low, high):
    level = 1.0
    for dim, blocks in pieces:
        heights = jax.random.uniform(jax.random.fold_in(jax.random.fold_in(stream_key, 6), dim), (blocks,), jnp.float32, low / len(pieces), high / len(pieces))
        level = level * jnp.repeat(jnp.exp(heights), dims[dim] // blocks).reshape((-1,) + (1,) * (len(dims) - 1 - dim))
    return level


def gaussian(rng, dims, deviation, bound, cuts=(), kind=jnp.bfloat16):
    factor_of = steps_of(rng, dims, cuts, -0.22, 0.18) if cuts else 1.0
    values = jax.random.normal(rng, dims, jnp.float32) * deviation * factor_of
    return jnp.minimum(jnp.maximum(values, -bound), bound).astype(kind)


def setup_inputs(seed: int = 0, part: int = 0) -> dict:
    splits = jax.random.split(jax.random.key(seed), 6)
    part_splits = jax.random.split(jax.random.fold_in(splits[5], part), 6)
    return {
        "state": gaussian(part_splits[0], (2, AMPS), 1.0, 6.0, ((1, 16),), jnp.float32),
        "unitaries": draw_unitaries(jax.random.fold_in(splits[5], 71), part),
        "gate_order": jax.random.permutation(splits[2], NGATES).astype(jnp.int32),
        "gate_starts": place_ends(jax.random.randint(splits[3], (NGATES,), 0, 2), jax.random.fold_in(splits[3], 1), 0, 1).astype(jnp.int32),
        "pair_gates": draw_pair_gates(jax.random.fold_in(splits[5], 71), part),
    }


HIGH = lax.Precision.HIGHEST

def mix(mat, vec):
    return jnp.einsum('ij,ajb->aib', mat, vec, precision=HIGH)

def dense_branch(re_part, im_part, u_re, u_im, offset):
    gdim = u_re.shape[0]
    gq = gdim.bit_length() - 1
    block = 2 ** (gq + offset)
    shaped_re = re_part.reshape(-1, gdim, block)
    shaped_im = im_part.reshape(-1, gdim, block)
    new_re = mix(u_re, shaped_re) - mix(u_im, shaped_im)
    new_im = mix(u_re, shaped_im) + mix(u_im, shaped_re)
    return (new_re.reshape(-1), new_im.reshape(-1))

def dense_gate(stacked, unitaries, gate_order, gate_starts, k):
    chosen = unitaries[gate_order[k]]
    branches = [partial(dense_branch, offset=0), partial(dense_branch, offset=1)]
    new_re, new_im = lax.switch(gate_starts[k], branches, stacked[0], stacked[1], chosen[0], chosen[1])
    return jnp.stack([new_re, new_im])

def one_qubit(stacked, gate, qubit):
    shaped = stacked.reshape(2, -1, 2, 2 ** qubit)
    u_re, u_im = (gate[0], gate[1])
    new_re = jnp.einsum('bc,acx->abx', u_re, shaped[0], precision=HIGH) - jnp.einsum('bc,acx->abx', u_im, shaped[1], precision=HIGH)
    new_im = jnp.einsum('bc,acx->abx', u_re, shaped[1], precision=HIGH) + jnp.einsum('bc,acx->abx', u_im, shaped[0], precision=HIGH)
    return jnp.stack([new_re, new_im]).reshape(2, -1)

def qubit_swap(stacked):
    shaped = stacked.reshape(2, QA_DEVS, QA_DEVS, AMP_DEV // QA_DEVS)
    return jnp.transpose(shaped, (0, 2, 1, 3)).reshape(2, -1)

def reference(state, unitaries, gate_order, gate_starts, pair_gates):
    local_bits = AMP_DEV.bit_length() - 1
    global_bits = QA_DEVS.bit_length() - 1
    third = NGATES // 3
    stacked = state
    for k in range(third):
        stacked = dense_gate(stacked, unitaries, gate_order, gate_starts, k)
    stacked = qubit_swap(stacked)
    stacked = one_qubit(stacked, pair_gates[0], local_bits + global_bits - 1)
    for k in range(third, 2 * third):
        stacked = dense_gate(stacked, unitaries, gate_order, gate_starts, k)
    stacked = qubit_swap(stacked)
    stacked = one_qubit(stacked, pair_gates[1], local_bits)
    for k in range(2 * third, NGATES):
        stacked = dense_gate(stacked, unitaries, gate_order, gate_starts, k)
    return stacked
```

```python
from functools import partial

import jax
import jax.numpy as jnp
from jax import lax
from jax.experimental import pallas as pl
from jax.experimental.pallas import tpu as pltpu
from jax.sharding import PartitionSpec as P

HIGH = lax.Precision.HIGHEST
F32 = jnp.float32
BF16 = jnp.bfloat16


def mix(mat, vec):
    return jnp.einsum("ij,ajb->aib", mat, vec, precision=HIGH)


def dense_branch(re_part, im_part, u_re, u_im, offset):
    gdim = u_re.shape[0]
    gq = gdim.bit_length() - 1
    block = 2 ** (gq + offset)
    shaped_re = re_part.reshape(-1, gdim, block)
    shaped_im = im_part.reshape(-1, gdim, block)
    new_re = mix(u_re, shaped_re) - mix(u_im, shaped_im)
    new_im = mix(u_re, shaped_im) + mix(u_im, shaped_re)
    return (new_re.reshape(-1), new_im.reshape(-1))


def dense_gate(stacked, unitaries, gate_order, gate_starts, k):
    chosen = unitaries[gate_order[k]]
    branches = [partial(dense_branch, offset=0), partial(dense_branch, offset=1)]
    new_re, new_im = lax.switch(
        gate_starts[k], branches, stacked[0], stacked[1], chosen[0], chosen[1]
    )
    return jnp.stack([new_re, new_im])


def one_qubit(stacked, gate, qubit):
    shaped = stacked.reshape(2, -1, 2, 2**qubit)
    u_re, u_im = (gate[0], gate[1])
    new_re = jnp.einsum("bc,acx->abx", u_re, shaped[0], precision=HIGH) - jnp.einsum(
        "bc,acx->abx", u_im, shaped[1], precision=HIGH
    )
    new_im = jnp.einsum("bc,acx->abx", u_re, shaped[1], precision=HIGH) + jnp.einsum(
        "bc,acx->abx", u_im, shaped[0], precision=HIGH
    )
    return jnp.stack([new_re, new_im]).reshape(2, -1)


def swap_qubits(stacked):
    devices = lax.axis_size("qa")
    shaped = stacked.reshape(2, devices, -1)
    moved = lax.all_to_all(shaped, "qa", split_axis=1, concat_axis=1, tiled=True)
    return moved.reshape(2, -1)


def general(state, unitaries, gate_order, gate_starts, pair_gates):
    local_bits = state.shape[1].bit_length() - 1
    global_bits = lax.axis_size("qa").bit_length() - 1
    ngates = unitaries.shape[0]
    third = ngates // 3
    stacked = state
    for k in range(third):
        stacked = dense_gate(stacked, unitaries, gate_order, gate_starts, k)
    stacked = one_qubit(stacked, pair_gates[0], local_bits - 1)
    stacked = swap_qubits(stacked)
    for k in range(third, 2 * third):
        stacked = dense_gate(stacked, unitaries, gate_order, gate_starts, k)
    stacked = one_qubit(stacked, pair_gates[1], local_bits - global_bits)
    stacked = swap_qubits(stacked)
    for k in range(2 * third, ngates):
        stacked = dense_gate(stacked, unitaries, gate_order, gate_starts, k)
    return stacked


def split(x):
    hi = x.astype(BF16)
    return hi, (x - hi.astype(F32)).astype(BF16)


def dot3(w_hi, w_lo, x):
    x_hi, x_lo = split(x)
    out = jnp.dot(w_hi, x_hi, preferred_element_type=F32)
    out += jnp.dot(w_hi, x_lo, preferred_element_type=F32)
    return out + jnp.dot(w_lo, x_hi, preferred_element_type=F32)


def embed(re, im):
    return jnp.concatenate(
        [jnp.concatenate([re, -im], axis=1), jnp.concatenate([im, re], axis=1)], axis=0
    )


def my_bits():
    me = lax.axis_index("qa")
    return lax.rem(me, 2), lax.rem(lax.div(me, 2), 2)


def compose(first, count, flip, order, starts, unit, m_re, m_im):
    gdim = unit.shape[-1]
    row = lax.broadcasted_iota(jnp.int32, (2 * gdim, 2 * gdim), 0)
    col = lax.broadcasted_iota(jnp.int32, (2 * gdim, 2 * gdim), 1)
    one = jnp.where(row == jnp.bitwise_xor(col, flip), 1.0, 0.0).astype(F32)
    for j in range(2):
        m_re[j] = one[:, j * gdim : (j + 1) * gdim]
    m_im[...] = jnp.zeros_like(m_im)

    def step(k, carry):
        gate = order[k]
        w_hi, w_lo = split(embed(unit[gate, 0], unit[gate, 1]))

        def run(rows):
            blocks = [(j, r) for r in rows for j in range(2)]
            x = jnp.concatenate(
                [jnp.concatenate([m_re[j, r, :], m_im[j, r, :]], axis=0) for j, r in blocks],
                axis=1,
            )
            y = dot3(w_hi, w_lo, x)
            for i, (j, r) in enumerate(blocks):
                m_re[j, r, :] = y[:gdim, gdim * i : gdim * (i + 1)]
                m_im[j, r, :] = y[gdim:, gdim * i : gdim * (i + 1)]

        @pl.when(starts[k] == 0)
        def _():
            run([pl.ds(b * gdim, gdim) for b in range(2)])

        @pl.when(starts[k] != 0)
        def _():
            run([pl.ds(b, gdim, stride=2) for b in range(2)])

        return carry

    lax.fori_loop(first, first + count, step, 0)


def whole(m):
    return jnp.concatenate([m[j] for j in range(2)], axis=1)


def parts_of(ref, at, rows):
    return jnp.concatenate(
        [ref[at, pl.ds(0, rows, stride=2), :], ref[at, pl.ds(1, rows, stride=2), :]], axis=0
    )


def front_kernel(count, order, starts, unit, state, w_ref, kept, m_re, m_im):
    compose(0, count, 0, order, starts, unit, m_re, m_im)
    w_hi, w_lo = split(embed(whole(m_re), whole(m_im)))
    w_ref[0] = w_hi
    w_ref[1] = w_lo
    _, h1 = my_bits()
    rows = state.shape[1] // 2
    x = jnp.concatenate([parts_of(state, h1 * 2 + c, rows) for c in range(2)], axis=1)
    y = dot3(w_hi, w_lo, x)
    lanes = state.shape[2]
    for c in range(2):
        kept[c] = y[:, c * lanes : (c + 1) * lanes]


def rest_kernel(count, order, starts, pair, unit, w1_ref, w2_ref, m_re, m_im):
    gdim = unit.shape[-1]
    half = gdim // 2
    h0, h1 = my_bits()
    compose(count, count, h1 * gdim + h0 * half, order, starts, unit, m_re, m_im)
    re, im = [], []
    for k in range(2):
        at = lax.rem(h1 + k, 2) * gdim
        r, i = 0.0, 0.0
        for b in range(2):
            rows = pl.ds(pl.multiple_of(at + b * half, half), half)
            v_re, v_im = pair[4 * 2 + h0 * 2 + b], pair[4 * 3 + h0 * 2 + b]
            x_re, x_im = (
                jnp.concatenate([m[j, rows, :] for j in range(2)], axis=1) for m in (m_re, m_im)
            )
            r += v_re * x_re - v_im * x_im
            i += v_re * x_im + v_im * x_re
        re.append(r)
        im.append(i)
    w_hi, w_lo = split(embed(jnp.concatenate(re, axis=0), jnp.concatenate(im, axis=0)))
    w1_ref[0] = w_hi
    w1_ref[1] = w_lo
    compose(2 * count, count, 0, order, starts, unit, m_re, m_im)
    w_hi, w_lo = split(embed(whole(m_re), whole(m_im)))
    w2_ref[0] = w_hi
    w2_ref[1] = w_lo


def first_kernel(w_ref, raw, out):
    rows = raw.shape[1] // 2
    out[0] = dot3(w_ref[0], w_ref[1], parts_of(raw, 0, rows))


def middle_kernel(w1_ref, w2_ref, own_kept, other_kept, own_came, other_came, keep, back):
    lanes = own_kept.shape[2]
    dim = own_kept.shape[1] // 2
    part = dim // 4
    sources = (own_kept, other_kept, own_came, other_came)
    cols = []
    for f in range(4):
        cols.append(
            jnp.concatenate(
                [s[0, pl.ds(p * dim + f * part, part), :] for p in range(2) for s in sources],
                axis=0,
            )
        )
    y = dot3(w1_ref[0], w1_ref[1], jnp.concatenate(cols, axis=1))
    cols = []
    for k in range(2):
        cols.append(
            jnp.concatenate(
                [
                    y[(2 * p + k) * part : (2 * p + k + 1) * part, f * lanes : (f + 1) * lanes]
                    for p in range(2)
                    for f in range(4)
                ],
                axis=0,
            )
        )
    z = dot3(w2_ref[0], w2_ref[1], jnp.concatenate(cols, axis=1))
    keep[0] = z[:, :lanes]
    back[0] = z[:, lanes:]


def last_kernel(pair, keep0, back0, keep1, back1, out):
    _, h1 = my_bits()
    rows = keep0.shape[1] // 2
    for c, (keep, back) in enumerate(((keep0, back0), (keep1, back1))):
        k_re, k_im = keep[0, :rows, :], keep[0, rows:, :]
        b_re, b_im = back[0, :rows, :], back[0, rows:, :]
        for b in range(2):
            v_re, v_im = pair[b * 2 + h1], pair[4 + b * 2 + h1]
            u_re, u_im = pair[b * 2 + 1 - h1], pair[4 + b * 2 + 1 - h1]
            at = b * 2 + c
            out[at, pl.ds(0, rows, stride=2), :] = (
                v_re * k_re - v_im * k_im + u_re * b_re - u_im * b_im
            )
            out[at, pl.ds(1, rows, stride=2), :] = (
                v_re * k_im + v_im * k_re + u_re * b_im + u_im * b_re
            )


def call(body, outs, args, specs, scratch=(), flops=0):
    nbytes = sum(a.size * a.dtype.itemsize for a in (*outs, *args))
    return pl.pallas_call(
        body,
        out_shape=outs,
        in_specs=specs,
        out_specs=[pl.BlockSpec(memory_space=pltpu.VMEM)] * len(outs),
        scratch_shapes=scratch,
        cost_estimate=pl.CostEstimate(flops=flops, bytes_accessed=nbytes, transcendentals=0),
    )(*args)


def paired(state, unitaries, gate_order, gate_starts, pair_gates):
    devices = lax.axis_size("qa")
    count = unitaries.shape[0] // 3
    gdim = unitaries.shape[-1]
    lanes = gdim
    rows = 4 * gdim
    dim = 2 * gdim
    vm = pl.BlockSpec(memory_space=pltpu.VMEM)
    sm = pl.BlockSpec(memory_space=pltpu.SMEM)
    f32 = partial(jax.ShapeDtypeStruct, dtype=F32)
    bf16 = partial(jax.ShapeDtypeStruct, dtype=BF16)
    _, h1 = my_bits()
    pair = pair_gates.reshape(-1)

    def other(v, bit):
        return lax.ppermute(v, "qa", [(i, i ^ bit) for i in range(devices)])

    view = state.reshape(2, -1, lanes).transpose(1, 0, 2).reshape(4, rows, lanes)
    came = [
        other(lax.dynamic_slice_in_dim(view, (1 - h1) * 2 + c, 1, axis=0), 2) for c in range(2)
    ]
    scratch = [pltpu.VMEM((2, dim, gdim), F32)] * 2
    step = 3 * 2 * (2 * gdim) * (2 * gdim) * (4 * gdim)
    w0, kept = call(
        partial(front_kernel, count),
        [bf16((2, rows, rows)), f32((2, rows, lanes))],
        [gate_order, gate_starts, unitaries, view],
        [sm, sm, vm, vm],
        scratch,
        flops=count * step + 6 * rows * rows * 2 * lanes,
    )
    kept = [kept[c : c + 1] for c in range(2)]
    kept_other = [other(k, 1) for k in kept]
    w1, w2 = call(
        partial(rest_kernel, count),
        [bf16((2, dim, rows)), bf16((2, rows, rows))],
        [gate_order, gate_starts, pair, unitaries],
        [sm, sm, sm, vm],
        scratch,
        flops=2 * count * step,
    )
    block = f32((1, rows, lanes))
    done = []
    for c in range(2):
        (mine,) = call(
            first_kernel, [block], [w0, came[c]], [vm, vm], flops=6 * rows * rows * lanes
        )
        theirs = other(mine, 1)
        keep, back = call(
            middle_kernel,
            [block, block],
            [w1, w2, kept[c], kept_other[c], mine, theirs],
            [vm] * 6,
            flops=6 * rows * rows * 4 * lanes,
        )
        done += [keep, other(back, 2)]
    (out,) = call(last_kernel, [f32((4, rows, lanes))], [pair, *done], [sm] + [vm] * 4)
    return out.reshape(-1, 2, lanes).transpose(1, 0, 2).reshape(2, -1)


def shards(state, unitaries, gate_order, gate_starts, pair_gates):
    local_bits = state.shape[1].bit_length() - 1
    global_bits = lax.axis_size("qa").bit_length() - 1
    gate_bits = unitaries.shape[-1].bit_length() - 1
    top = 2 * gate_bits + 1
    met = top - (local_bits - global_bits)
    args = (state, unitaries, gate_order, gate_starts, pair_gates)
    if met == 2 and local_bits == top + 2 and global_bits >= 2:
        return paired(*args)
    return general(*args)


def solution(mesh):
    placed = (P(None, ("cuts", "qa")), P(), P(), P(), P())
    return jax.shard_map(
        shards, mesh=mesh, in_specs=placed, out_specs=P(None, ("cuts", "qa")), check_vma=False
    )
```

```python
from functools import partial

import jax
import jax.numpy as jnp
from jax import lax
from jax.experimental import pallas as pl
from jax.experimental.pallas import tpu as pltpu
from jax.sharding import PartitionSpec as P


HIGH = lax.Precision.HIGHEST
F32 = jnp.float32
BF16 = jnp.bfloat16


def mix(mat, vec):
    return jnp.einsum("ij,ajb->aib", mat, vec, precision=HIGH)


def dense_branch(re_part, im_part, u_re, u_im, offset):
    gdim = u_re.shape[0]
    gq = gdim.bit_length() - 1
    block = 2 ** (gq + offset)
    shaped_re = re_part.reshape(-1, gdim, block)
    shaped_im = im_part.reshape(-1, gdim, block)
    new_re = mix(u_re, shaped_re) - mix(u_im, shaped_im)
    new_im = mix(u_re, shaped_im) + mix(u_im, shaped_re)
    return (new_re.reshape(-1), new_im.reshape(-1))


def dense_gate(stacked, unitaries, gate_order, gate_starts, k):
    chosen = unitaries[gate_order[k]]
    branches = [partial(dense_branch, offset=0), partial(dense_branch, offset=1)]
    new_re, new_im = lax.switch(
        gate_starts[k], branches, stacked[0], stacked[1], chosen[0], chosen[1]
    )
    return jnp.stack([new_re, new_im])


def one_qubit(stacked, gate, qubit):
    shaped = stacked.reshape(2, -1, 2, 2**qubit)
    u_re, u_im = (gate[0], gate[1])
    new_re = jnp.einsum("bc,acx->abx", u_re, shaped[0], precision=HIGH) - jnp.einsum(
        "bc,acx->abx", u_im, shaped[1], precision=HIGH
    )
    new_im = jnp.einsum("bc,acx->abx", u_re, shaped[1], precision=HIGH) + jnp.einsum(
        "bc,acx->abx", u_im, shaped[0], precision=HIGH
    )
    return jnp.stack([new_re, new_im]).reshape(2, -1)


def swap_qubits(stacked):
    devices = lax.axis_size("qa")
    shaped = stacked.reshape(2, devices, -1)
    moved = lax.all_to_all(shaped, "qa", split_axis=1, concat_axis=1, tiled=True)
    return moved.reshape(2, -1)


def general(state, unitaries, gate_order, gate_starts, pair_gates):
    local_bits = state.shape[1].bit_length() - 1
    global_bits = lax.axis_size("qa").bit_length() - 1
    ngates = unitaries.shape[0]
    third = ngates // 3
    stacked = state
    for k in range(third):
        stacked = dense_gate(stacked, unitaries, gate_order, gate_starts, k)
    stacked = one_qubit(stacked, pair_gates[0], local_bits - 1)
    stacked = swap_qubits(stacked)
    for k in range(third, 2 * third):
        stacked = dense_gate(stacked, unitaries, gate_order, gate_starts, k)
    stacked = one_qubit(stacked, pair_gates[1], local_bits - global_bits)
    stacked = swap_qubits(stacked)
    for k in range(2 * third, ngates):
        stacked = dense_gate(stacked, unitaries, gate_order, gate_starts, k)
    return stacked


def split(x):
    hi = x.astype(BF16)
    return hi, (x - hi.astype(F32)).astype(BF16)


def dot3(w_hi, w_lo, x):
    x_hi, x_lo = split(x)
    return jnp.dot(
        jnp.concatenate([w_hi, w_hi, w_lo], axis=1),
        jnp.concatenate([x_hi, x_lo, x_hi], axis=0),
        preferred_element_type=F32,
    )


def embed(re, im):
    return jnp.concatenate(
        [jnp.concatenate([re, -im], axis=1), jnp.concatenate([im, re], axis=1)], axis=0
    )


def my_bits():
    me = lax.axis_index("qa")
    return lax.rem(me, 2), lax.rem(lax.div(me, 2), 2)


def compose(first, count, flip, order, starts, unit, m_re, m_im):
    gdim = unit.shape[-1]
    row = lax.broadcasted_iota(jnp.int32, (2 * gdim, 2 * gdim), 0)
    col = lax.broadcasted_iota(jnp.int32, (2 * gdim, 2 * gdim), 1)
    one = jnp.where(row == jnp.bitwise_xor(col, flip), 1.0, 0.0).astype(F32)
    for j in range(2):
        m_re[j] = one[:, j * gdim : (j + 1) * gdim]
    m_im[...] = jnp.zeros_like(m_im)

    def step(k, carry):
        gate = order[k]
        w_hi, w_lo = split(embed(unit[gate, 0], unit[gate, 1]))

        def run(rows):
            blocks = [(j, r) for r in rows for j in range(2)]
            x = jnp.concatenate(
                [jnp.concatenate([m_re[j, r, :], m_im[j, r, :]], axis=0) for j, r in blocks],
                axis=1,
            )
            y = dot3(w_hi, w_lo, x)
            for i, (j, r) in enumerate(blocks):
                m_re[j, r, :] = y[:gdim, gdim * i : gdim * (i + 1)]
                m_im[j, r, :] = y[gdim:, gdim * i : gdim * (i + 1)]

        @pl.when(starts[k] == 0)
        def _():
            run([pl.ds(b * gdim, gdim) for b in range(2)])

        @pl.when(starts[k] != 0)
        def _():
            run([pl.ds(b, gdim, stride=2) for b in range(2)])

        return carry

    lax.fori_loop(first, first + count, step, 0)


def put(ref, re, im):
    ref[0], ref[1] = split(embed(re, im))


def whole(m):
    return jnp.concatenate([m[j] for j in range(2)], axis=1)


def parts_of(ref, at, rows):
    return jnp.concatenate(
        [ref[at, pl.ds(0, rows, stride=2), :], ref[at, pl.ds(1, rows, stride=2), :]], axis=0
    )


def front_kernel(count, order, starts, unit, state, w_ref, kept0, kept1, m_re, m_im, u, s, sems):
    _, h1 = my_bits()
    copies = [
        pltpu.make_async_copy(unit, u, sems.at[0]),
        pltpu.make_async_copy(state.at[pl.ds(h1 * 2, 2)], s, sems.at[1]),
    ]
    for c in copies:
        c.start()
    copies[0].wait()
    compose(0, count, 0, order, starts, u, m_re, m_im)
    put(w_ref, whole(m_re), whole(m_im))
    copies[1].wait()
    rows = s.shape[1] // 2
    x = jnp.concatenate([parts_of(s, c, rows) for c in range(2)], axis=1)
    y = dot3(w_ref[0], w_ref[1], x)
    lanes = s.shape[2]
    kept0[0] = y[:, :lanes]
    kept1[0] = y[:, lanes:]


def second_kernel(count, order, starts, pair, unit, w_ref, m_re, m_im):
    gdim = unit.shape[-1]
    half = gdim // 2
    h0, h1 = my_bits()
    compose(count, count, h1 * gdim + h0 * half, order, starts, unit, m_re, m_im)
    re, im = [], []
    for k in range(2):
        at = lax.rem(h1 + k, 2) * gdim
        r, i = 0.0, 0.0
        for b in range(2):
            rows = pl.ds(pl.multiple_of(at + b * half, half), half)
            v_re, v_im = pair[1, 0, h0, b], pair[1, 1, h0, b]
            x_re, x_im = (
                jnp.concatenate([m[j, rows, :] for j in range(2)], axis=1) for m in (m_re, m_im)
            )
            r += v_re * x_re - v_im * x_im
            i += v_re * x_im + v_im * x_re
        re.append(r)
        im.append(i)
    put(w_ref, jnp.concatenate(re, axis=0), jnp.concatenate(im, axis=0))


def third_kernel(count, order, starts, unit, w_ref, m_re, m_im):
    compose(2 * count, count, 0, order, starts, unit, m_re, m_im)
    put(w_ref, whole(m_re), whole(m_im))


def first_kernel(w_ref, raw, out):
    rows = raw.shape[1] // 2
    out[0] = dot3(w_ref[0], w_ref[1], parts_of(raw, 0, rows))


def middle_kernel(w1_ref, w2_ref, own_kept, other_kept, own_came, other_came, keep, back):
    lanes = own_kept.shape[2]
    dim = own_kept.shape[1] // 2
    part = dim // 4
    sources = (own_kept, other_kept, own_came, other_came)
    cols = []
    for f in range(4):
        cols.append(
            jnp.concatenate(
                [s[0, pl.ds(p * dim + f * part, part), :] for p in range(2) for s in sources],
                axis=0,
            )
        )
    y = dot3(w1_ref[0], w1_ref[1], jnp.concatenate(cols, axis=1))
    cols = []
    for k in range(2):
        cols.append(
            jnp.concatenate(
                [
                    y[(2 * p + k) * part : (2 * p + k + 1) * part, f * lanes : (f + 1) * lanes]
                    for p in range(2)
                    for f in range(4)
                ],
                axis=0,
            )
        )
    z = dot3(w2_ref[0], w2_ref[1], jnp.concatenate(cols, axis=1))
    keep[0] = z[:, :lanes]
    back[0] = z[:, lanes:]


def last_kernel(pair, keep, back, *refs):
    out = refs[-1]
    _, h1 = my_bits()
    b = pl.program_id(0)
    rows = keep.shape[1] // 2
    k_re, k_im = keep[0, :rows, :], keep[0, rows:, :]
    b_re, b_im = back[0, :rows, :], back[0, rows:, :]
    v_re, v_im = pair[0, 0, b, h1], pair[0, 1, b, h1]
    u_re, u_im = pair[0, 0, b, 1 - h1], pair[0, 1, b, 1 - h1]
    out[0, 0, pl.ds(0, rows, stride=2), :] = v_re * k_re - v_im * k_im + u_re * b_re - u_im * b_im
    out[0, 0, pl.ds(1, rows, stride=2), :] = v_re * k_im + v_im * k_re + u_re * b_im + u_im * b_re


VM = pl.BlockSpec(memory_space=pltpu.VMEM)
SM = pl.BlockSpec(memory_space=pltpu.SMEM)
HB = pl.BlockSpec(memory_space=pltpu.HBM)


def cost(outs, args, flops):
    nbytes = sum(a.size * a.dtype.itemsize for a in (*outs, *args))
    return pl.CostEstimate(flops=flops, bytes_accessed=nbytes, transcendentals=0)


PARAMS = pltpu.CompilerParams(vmem_limit_bytes=16 * 2**20)


def call(body, outs, args, specs, scratch=(), flops=0):
    return pl.pallas_call(
        body,
        out_shape=outs,
        in_specs=specs,
        out_specs=[VM] * len(outs),
        scratch_shapes=scratch,
        cost_estimate=cost(outs, args, flops),
        compiler_params=PARAMS,
    )(*args)


def finish(pair, keep, back, shape, chunk, before=None):
    args = [pair, keep, back] + ([] if before is None else [before])
    return pl.pallas_call(
        last_kernel,
        out_shape=shape,
        grid=(2,),
        in_specs=[SM, VM, VM] + ([] if before is None else [HB]),
        out_specs=pl.BlockSpec((1, 1, *shape.shape[2:]), lambda i: (i, chunk, 0, 0)),
        input_output_aliases={} if before is None else {3: 0},
        cost_estimate=cost([shape], [keep, back], 0),
        compiler_params=PARAMS,
    )(*args)


def paired(state, unitaries, gate_order, gate_starts, pair):
    devices = lax.axis_size("qa")
    count = unitaries.shape[0] // 3
    gdim = unitaries.shape[-1]
    lanes, rows, dim = gdim, 4 * gdim, 2 * gdim
    f32 = partial(jax.ShapeDtypeStruct, dtype=F32)
    bf16 = partial(jax.ShapeDtypeStruct, dtype=BF16)
    tie = lax.optimization_barrier
    far = partial(pltpu.with_memory_space_constraint, memory_space=pltpu.HBM)
    _, h1 = my_bits()

    def other(v, bit):
        return lax.ppermute(v, "qa", [(i, i ^ bit) for i in range(devices)])

    def block_of(v, c):
        return lax.dynamic_slice_in_dim(v, (1 - h1) * 2 + c, 1, axis=0)

    view = state.reshape(2, -1, lanes).transpose(1, 0, 2).reshape(4, rows, lanes)
    came = [other(block_of(view, c), 2) for c in range(2)]
    scratch = [pltpu.VMEM((2, dim, gdim), F32)] * 2
    step = 3 * 2 * (2 * gdim) * (2 * gdim) * (4 * gdim)
    block = f32((1, rows, lanes))
    w0, *kept = call(
        partial(front_kernel, count),
        [bf16((2, rows, rows)), block, block],
        [far(gate_order), far(gate_starts), far(unitaries), far(view)],
        [SM, SM, HB, HB],
        scratch
        + [
            pltpu.VMEM(unitaries.shape, F32),
            pltpu.VMEM((2, rows, lanes), F32),
            pltpu.SemaphoreType.DMA((2,)),
        ],
        flops=count * step + 6 * rows * rows * 2 * lanes,
    )
    kept_other = [other(k, 1) for k in kept]
    (w1,) = call(
        partial(second_kernel, count),
        [bf16((2, dim, rows))],
        [gate_order, gate_starts, pair, unitaries],
        [SM, SM, SM, VM],
        scratch,
        flops=count * step,
    )

    def enter(v):
        flops = 6 * rows * rows * lanes
        return call(first_kernel, [block], [w0, v], [VM, VM], flops=flops)[0]

    def middle(c, mine):
        return call(
            middle_kernel,
            [block, block],
            [w1, w2, kept[c], kept_other[c], mine, other(mine, 1)],
            [VM] * 6,
            flops=6 * rows * rows * 4 * lanes,
        )

    came[0], w1 = tie((came[0], w1))
    mine = enter(came[0])
    order_then, mine = tie((gate_order, mine))
    (w2,) = call(
        partial(third_kernel, count),
        [bf16((2, rows, rows))],
        [order_then, gate_starts, unitaries],
        [SM, SM, VM],
        scratch,
        flops=count * step,
    )
    keep0, back0 = middle(0, mine)
    came[1], back0 = tie((came[1], back0))
    back0 = other(back0, 2)
    keep1, back1 = middle(1, enter(came[1]))
    back0, keep1 = tie((back0, keep1))
    back1 = other(back1, 2)
    whole_shape = f32((2, 2, rows, lanes))
    out = finish(pair, keep0, back0, whole_shape, 0)
    out = finish(pair, keep1, back1, whole_shape, 1, out)
    return out.reshape(-1, 2, lanes).transpose(1, 0, 2).reshape(2, -1)


def meets_two(state, unitaries, devices):
    local_bits = state.shape[1].bit_length() - 1
    global_bits = devices.bit_length() - 1
    top = 2 * (unitaries.shape[-1].bit_length() - 1) + 1
    met = top - (local_bits - global_bits)
    return met == 2 and local_bits == top + 2 and global_bits >= 2


def shards(*args):
    if meets_two(args[0], args[1], lax.axis_size("qa")):
        return paired(*args)
    return general(*args)


def solution(mesh):
    placed = (P(None, ("cuts", "qa")), P(), P(), P(), P())
    return jax.shard_map(
        shards, mesh=mesh, in_specs=placed, out_specs=P(None, ("cuts", "qa")), check_vma=False
    )
```

```python
from functools import partial

import jax
import jax.numpy as jnp
from jax import lax
from jax.experimental import pallas as pl
from jax.experimental.pallas import tpu as pltpu
from jax.sharding import PartitionSpec as P


HIGH = lax.Precision.HIGHEST
F32 = jnp.float32
BF16 = jnp.bfloat16


def mix(mat, vec):
    return jnp.einsum("ij,ajb->aib", mat, vec, precision=HIGH)


def dense_branch(re_part, im_part, u_re, u_im, offset):
    gdim = u_re.shape[0]
    gq = gdim.bit_length() - 1
    block = 2 ** (gq + offset)
    shaped_re = re_part.reshape(-1, gdim, block)
    shaped_im = im_part.reshape(-1, gdim, block)
    new_re = mix(u_re, shaped_re) - mix(u_im, shaped_im)
    new_im = mix(u_re, shaped_im) + mix(u_im, shaped_re)
    return (new_re.reshape(-1), new_im.reshape(-1))


def dense_gate(stacked, unitaries, gate_order, gate_starts, k):
    chosen = unitaries[gate_order[k]]
    branches = [partial(dense_branch, offset=0), partial(dense_branch, offset=1)]
    new_re, new_im = lax.switch(
        gate_starts[k], branches, stacked[0], stacked[1], chosen[0], chosen[1]
    )
    return jnp.stack([new_re, new_im])


def one_qubit(stacked, gate, qubit):
    shaped = stacked.reshape(2, -1, 2, 2**qubit)
    u_re, u_im = (gate[0], gate[1])
    new_re = jnp.einsum("bc,acx->abx", u_re, shaped[0], precision=HIGH) - jnp.einsum(
        "bc,acx->abx", u_im, shaped[1], precision=HIGH
    )
    new_im = jnp.einsum("bc,acx->abx", u_re, shaped[1], precision=HIGH) + jnp.einsum(
        "bc,acx->abx", u_im, shaped[0], precision=HIGH
    )
    return jnp.stack([new_re, new_im]).reshape(2, -1)


def swap_qubits(stacked):
    devices = lax.axis_size("qa")
    shaped = stacked.reshape(2, devices, -1)
    moved = lax.all_to_all(shaped, "qa", split_axis=1, concat_axis=1, tiled=True)
    return moved.reshape(2, -1)


def general(state, unitaries, gate_order, gate_starts, pair_gates):
    local_bits = state.shape[1].bit_length() - 1
    global_bits = lax.axis_size("qa").bit_length() - 1
    ngates = unitaries.shape[0]
    third = ngates // 3
    stacked = state
    for k in range(third):
        stacked = dense_gate(stacked, unitaries, gate_order, gate_starts, k)
    stacked = one_qubit(stacked, pair_gates[0], local_bits - 1)
    stacked = swap_qubits(stacked)
    for k in range(third, 2 * third):
        stacked = dense_gate(stacked, unitaries, gate_order, gate_starts, k)
    stacked = one_qubit(stacked, pair_gates[1], local_bits - global_bits)
    stacked = swap_qubits(stacked)
    for k in range(2 * third, ngates):
        stacked = dense_gate(stacked, unitaries, gate_order, gate_starts, k)
    return stacked


def split(x):
    hi = x.astype(BF16)
    return hi, (x - hi.astype(F32)).astype(BF16)


def dot3(w_hi, w_lo, x):
    x_hi, x_lo = split(x)
    return jnp.dot(
        jnp.concatenate([w_hi, w_hi, w_lo], axis=1),
        jnp.concatenate([x_hi, x_lo, x_hi], axis=0),
        preferred_element_type=F32,
    )


def embed(re, im):
    return jnp.concatenate(
        [jnp.concatenate([re, -im], axis=1), jnp.concatenate([im, re], axis=1)], axis=0
    )


def my_bits():
    me = lax.axis_index("qa")
    return lax.rem(me, 2), lax.rem(lax.div(me, 2), 2)


def halves(gdim, start):
    if start == 0:
        return [pl.ds(b * gdim, gdim) for b in range(2)]
    return [pl.ds(b, gdim, stride=2) for b in range(2)]


def begin(k, flip, order, starts, unit, m):
    gdim = unit.shape[-1]
    gate, off = order[k], starts[k]
    row = lax.broadcasted_iota(jnp.int32, (gdim, 2 * gdim), 0)
    col = jnp.bitwise_xor(lax.broadcasted_iota(jnp.int32, (gdim, 2 * gdim), 1), flip)
    ones = jnp.concatenate(
        [
            jnp.where(row * (1 + off) + b * (gdim - off * (gdim - 1)) == col, 1.0, 0.0)
            for b in range(2)
        ],
        axis=1,
    ).astype(BF16)
    w_hi, w_lo = split(jnp.concatenate([unit[gate, 0], unit[gate, 1]], axis=0))
    y = jnp.dot(
        jnp.concatenate([w_hi, w_lo], axis=1),
        jnp.concatenate([ones, ones], axis=0),
        preferred_element_type=F32,
    )
    for start in range(2):

        @pl.when(off == start)
        def _():
            store(m, [(r, j) for r in halves(gdim, start) for j in range(2)], y)


def store(m, blocks, y):
    gdim = y.shape[0] // 2
    for i, (r, j) in enumerate(blocks):
        for p in range(2):
            m[p][j, r, :] = y[p * gdim : (p + 1) * gdim, gdim * i : gdim * (i + 1)]


def apply(k, order, starts, unit, source, m):
    gdim = unit.shape[-1]
    gate = order[k]
    w_hi, w_lo = split(embed(unit[gate, 0], unit[gate, 1]))
    for start in range(2):

        @pl.when(starts[k] == start)
        def _():
            blocks = [(r, j) for r in halves(gdim, start) for j in range(2)]
            x = jnp.concatenate(
                [jnp.concatenate([v[j, r, :] for v in source], axis=0) for r, j in blocks],
                axis=1,
            )
            store(m, blocks, dot3(w_hi, w_lo, x))


def compose(first, count, flip, order, starts, unit, m):
    begin(first, flip, order, starts, unit, m)

    def step(k, carry):
        apply(k, order, starts, unit, m, m)
        return carry

    lax.fori_loop(first + 1, first + count, step, 0)


def put(ref, re, im):
    ref[0], ref[1] = split(embed(re, im))


def whole(m):
    return jnp.concatenate([m[j] for j in range(2)], axis=1)


def parts_of(ref, at, rows):
    return jnp.concatenate(
        [ref[at, pl.ds(0, rows, stride=2), :], ref[at, pl.ds(1, rows, stride=2), :]], axis=0
    )


def front_kernel(count, order, starts, pair, unit, w0_ref, w1_ref, re_ref, im_ref, *scratch):
    order_s, starts_s, u, m_re, m_im, sems = scratch
    gdim = unit.shape[-1]
    half = gdim // 2
    h0, h1 = my_bits()
    pairs = ((order, order_s), (starts, starts_s), (unit, u))
    copies = [pltpu.make_async_copy(a, b, sems.at[i]) for i, (a, b) in enumerate(pairs)]
    for c in copies:
        c.start()
    for c in copies:
        c.wait()
    compose(0, count, 0, order_s, starts_s, u, (m_re, m_im))
    put(w0_ref, whole(m_re), whole(m_im))
    compose(count, count, h1 * gdim + h0 * half, order_s, starts_s, u, (m_re, m_im))
    re, im = [], []
    for k in range(2):
        at = lax.rem(h1 + k, 2) * gdim
        r, i = 0.0, 0.0
        for b in range(2):
            rows = pl.ds(pl.multiple_of(at + b * half, half), half)
            v_re, v_im = pair[1, 0, h0, b], pair[1, 1, h0, b]
            x_re, x_im = (
                jnp.concatenate([m[j, rows, :] for j in range(2)], axis=1) for m in (m_re, m_im)
            )
            r += v_re * x_re - v_im * x_im
            i += v_re * x_im + v_im * x_re
        re.append(r)
        im.append(i)
    put(w1_ref, jnp.concatenate(re, axis=0), jnp.concatenate(im, axis=0))
    compose(2 * count, count // 2, 0, order_s, starts_s, u, (re_ref, im_ref))


def third_kernel(count, order, starts, unit, re, im, w_ref, m_re, m_im):
    m = (m_re, m_im)
    source = (re, im)
    for k in range(2 * count + count // 2, 3 * count):
        apply(k, order, starts, unit, source, m)
        source = m
    put(w_ref, whole(source[0]), whole(source[1]))


def kept_kernel(chunk, w_ref, state, out):
    _, h1 = my_bits()
    rows = state.shape[1] // 2
    out[0] = dot3(w_ref[0], w_ref[1], parts_of(state, h1 * 2 + chunk, rows))


def came_kernel(w_ref, raw, out):
    out[0] = dot3(w_ref[0], w_ref[1], parts_of(raw, 0, raw.shape[1] // 2))


def enter_kernel(chunk, w_ref, state, raw, out):
    _, h1 = my_bits()
    rows, lanes = raw.shape[1] // 2, raw.shape[2]
    x = jnp.concatenate([parts_of(state, h1 * 2 + chunk, rows), parts_of(raw, 0, rows)], axis=1)
    y = dot3(w_ref[0], w_ref[1], x)
    out[0] = y[:, :lanes]
    out[1] = y[:, lanes:]


def middle_kernel(count, w1_ref, w2_ref, *refs):
    blocks, (keep, back) = refs[:count], refs[count:]
    lanes = back.shape[2]
    dim = back.shape[1] // 2
    part = dim // 4
    sources = [(v, k) for v in blocks for k in range(v.shape[0])]
    if count == 2:
        sources = [sources[0], sources[2], sources[1], sources[3]]
    cols = []
    for f in range(4):
        cols.append(
            jnp.concatenate(
                [v[k, pl.ds(p * dim + f * part, part), :] for p in range(2) for v, k in sources],
                axis=0,
            )
        )
    y = dot3(w1_ref[0], w1_ref[1], jnp.concatenate(cols, axis=1))
    cols = []
    for k in range(2):
        cols.append(
            jnp.concatenate(
                [
                    y[(2 * p + k) * part : (2 * p + k + 1) * part, f * lanes : (f + 1) * lanes]
                    for p in range(2)
                    for f in range(4)
                ],
                axis=0,
            )
        )
    z = dot3(w2_ref[0], w2_ref[1], jnp.concatenate(cols, axis=1))
    keep[0] = z[:, :lanes]
    back[0] = z[:, lanes:]


def scale_kernel(pair, keep, part0, part1, coef):
    _, h1 = my_bits()
    dim = keep.shape[1] // 2
    k_re, k_im = keep[0, :dim, :], keep[0, dim:, :]
    for b, out in enumerate((part0, part1)):
        v_re, v_im = pair[0, 0, b, h1], pair[0, 1, b, h1]
        out[0, :dim, :] = v_re * k_re - v_im * k_im
        out[0, dim:, :] = v_re * k_im + v_im * k_re
        for p in range(2):
            coef[b, p] = jnp.full(coef.shape[2:], pair[0, p, b, 1 - h1], F32)


def last_kernel(chunk, part0, part1, back, coef, *refs):
    out, buf, sems = refs[-3:]
    rows = back.shape[1] // 2
    cut = rows // 2
    copies = []
    for b, part in enumerate((part0, part1)):
        for q in range(2):
            at = q * cut
            u_re, u_im = coef[b, 0][:1], coef[b, 1][:1]
            re, im = pl.ds(at, cut), pl.ds(rows + at, cut)
            b_re, b_im = back[0, re, :], back[0, im, :]
            buf[b, pl.ds(2 * at, cut, stride=2), :] = part[0, re, :] + (u_re * b_re - u_im * b_im)
            buf[b, pl.ds(2 * at + 1, cut, stride=2), :] = part[0, im, :] + (u_re * b_im + u_im * b_re)
            span = pl.ds(2 * at, 2 * cut)
            copies.append(
                pltpu.make_async_copy(
                    buf.at[b, span], out.at[b, chunk, span], sems.at[2 * b + q]
                )
            )
            copies[-1].start()
    for c in copies:
        c.wait()


VM = pl.BlockSpec(memory_space=pltpu.VMEM)
SM = pl.BlockSpec(memory_space=pltpu.SMEM)
HB = pl.BlockSpec(memory_space=pltpu.HBM)


def cost(outs, args, flops):
    nbytes = sum(a.size * a.dtype.itemsize for a in (*outs, *args))
    return pl.CostEstimate(flops=flops, bytes_accessed=nbytes, transcendentals=0)


PARAMS = pltpu.CompilerParams(vmem_limit_bytes=16 * 2**20)


def call(body, outs, args, specs, scratch=(), flops=0):
    return pl.pallas_call(
        body,
        out_shape=outs,
        in_specs=specs,
        out_specs=[VM] * len(outs),
        scratch_shapes=scratch,
        cost_estimate=cost(outs, args, flops),
        compiler_params=PARAMS,
    )(*args)


def finish(args, shape, chunk, before=None):
    args = args + ([] if before is None else [before])
    return pl.pallas_call(
        partial(last_kernel, chunk),
        out_shape=shape,
        in_specs=[VM] * 4 + [HB] * (len(args) - 4),
        out_specs=HB,
        input_output_aliases={} if before is None else {4: 0},
        scratch_shapes=[pltpu.VMEM((2, *shape.shape[2:]), F32), pltpu.SemaphoreType.DMA((4,))],
        cost_estimate=cost([shape], args[:3], 0),
        compiler_params=PARAMS,
    )(*args)


def paired(state, unitaries, gate_order, gate_starts, pair):
    devices = lax.axis_size("qa")
    count = unitaries.shape[0] // 3
    gdim = unitaries.shape[-1]
    lanes, rows, dim = gdim, 4 * gdim, 2 * gdim
    f32 = partial(jax.ShapeDtypeStruct, dtype=F32)
    bf16 = partial(jax.ShapeDtypeStruct, dtype=BF16)
    tie = lax.optimization_barrier
    far = partial(pltpu.with_memory_space_constraint, memory_space=pltpu.HBM)
    _, h1 = my_bits()

    def other(v, bit):
        return lax.ppermute(v, "qa", [(i, i ^ bit) for i in range(devices)])

    def block_of(v, c):
        return lax.dynamic_slice_in_dim(v, (1 - h1) * 2 + c, 1, axis=0)

    view = state.reshape(2, -1, lanes).transpose(1, 0, 2).reshape(4, rows, lanes)
    came = [other(block_of(view, c), 2) for c in range(2)]
    step = 3 * 2 * (2 * gdim) * (2 * gdim) * (4 * gdim)
    enter_flops = 6 * rows * rows * lanes
    block, both, coef = f32((1, rows, lanes)), f32((2, rows, lanes)), f32((2, 2, 8, lanes))
    m = f32((2, dim, gdim))
    m_scratch = pltpu.VMEM(m.shape, F32)
    gates = [gate_order, gate_starts]
    w0, w1, re2, im2 = call(
        partial(front_kernel, count),
        [bf16((2, rows, rows)), bf16((2, dim, rows)), m, m],
        [far(v) for v in (*gates, pair, unitaries)],
        [HB, HB, SM, HB],
        [pltpu.SMEM(gate_order.shape, jnp.int32)] * 2
        + [pltpu.VMEM(unitaries.shape, F32), m_scratch, m_scratch, pltpu.SemaphoreType.DMA((3,))],
        flops=5 * count * step // 2,
    )
    (kept,) = call(partial(kept_kernel, 0), [block], [w0, view], [VM] * 2, flops=enter_flops)
    kept_other = other(kept, 1)
    re2, kept = tie((re2, kept))
    came[0], re2 = tie((came[0], re2))
    (mine,) = call(came_kernel, [block], [w0, came[0]], [VM] * 2, flops=enter_flops)
    re2, mine = tie((re2, mine))
    (w2,) = call(
        partial(third_kernel, count),
        [bf16((2, rows, rows))],
        [*gates, unitaries, re2, im2],
        [SM] * 2 + [VM] * 3,
        [m_scratch, m_scratch],
        flops=count * step // 2,
    )

    def middle(blocks):
        return call(
            partial(middle_kernel, len(blocks)),
            [block, block],
            [w1, w2, *blocks],
            [VM] * (2 + len(blocks)),
            flops=4 * enter_flops,
        )

    def scale(keep):
        return call(scale_kernel, [block, block, coef], [pair, keep], [SM, VM])

    shape = f32((2, 2, rows, lanes))
    keep0, back0 = middle([kept, kept_other, mine, other(mine, 1)])
    back0 = other(back0, 2)
    (mine,) = call(
        partial(enter_kernel, 1), [both], [w0, view, came[1]], [VM] * 3, flops=2 * enter_flops
    )
    theirs = other(mine, 1)
    mine, keep0 = tie((mine, keep0))
    keep0 = scale(keep0)
    keep1, back1 = middle([mine, theirs])
    back0, keep1 = tie((back0, keep1))
    back1 = other(back1, 2)
    *keep1, coef1 = scale(keep1)
    out = finish([*keep0[:2], back0, keep0[2]], shape, 0)
    out = finish([*keep1, back1, coef1], shape, 1, out)
    return out.reshape(-1, 2, lanes).transpose(1, 0, 2).reshape(2, -1)


def meets_two(state, unitaries, devices):
    local_bits = state.shape[1].bit_length() - 1
    global_bits = devices.bit_length() - 1
    top = 2 * (unitaries.shape[-1].bit_length() - 1) + 1
    met = top - (local_bits - global_bits)
    return met == 2 and local_bits == top + 2 and global_bits >= 2


def shards(*args):
    if meets_two(args[0], args[1], lax.axis_size("qa")):
        return paired(*args)
    return general(*args)


def solution(mesh):
    placed = (P(None, ("cuts", "qa")), P(), P(), P(), P())
    return jax.shard_map(
        shards, mesh=mesh, in_specs=placed, out_specs=P(None, ("cuts", "qa")), check_vma=False
    )
```

```python
from functools import partial

import jax
import jax.numpy as jnp
from jax import lax
from jax.experimental import pallas as pl
from jax.experimental.pallas import tpu as pltpu
from jax.sharding import PartitionSpec as P


HIGH = lax.Precision.HIGHEST
F32 = jnp.float32
BF16 = jnp.bfloat16


def mix(mat, vec):
    return jnp.einsum("ij,ajb->aib", mat, vec, precision=HIGH)


def dense_branch(re_part, im_part, u_re, u_im, offset):
    gdim = u_re.shape[0]
    gq = gdim.bit_length() - 1
    block = 2 ** (gq + offset)
    shaped_re = re_part.reshape(-1, gdim, block)
    shaped_im = im_part.reshape(-1, gdim, block)
    new_re = mix(u_re, shaped_re) - mix(u_im, shaped_im)
    new_im = mix(u_re, shaped_im) + mix(u_im, shaped_re)
    return (new_re.reshape(-1), new_im.reshape(-1))


def dense_gate(stacked, unitaries, gate_order, gate_starts, k):
    chosen = unitaries[gate_order[k]]
    branches = [partial(dense_branch, offset=0), partial(dense_branch, offset=1)]
    new_re, new_im = lax.switch(
        gate_starts[k], branches, stacked[0], stacked[1], chosen[0], chosen[1]
    )
    return jnp.stack([new_re, new_im])


def one_qubit(stacked, gate, qubit):
    shaped = stacked.reshape(2, -1, 2, 2**qubit)
    u_re, u_im = (gate[0], gate[1])
    new_re = jnp.einsum("bc,acx->abx", u_re, shaped[0], precision=HIGH) - jnp.einsum(
        "bc,acx->abx", u_im, shaped[1], precision=HIGH
    )
    new_im = jnp.einsum("bc,acx->abx", u_re, shaped[1], precision=HIGH) + jnp.einsum(
        "bc,acx->abx", u_im, shaped[0], precision=HIGH
    )
    return jnp.stack([new_re, new_im]).reshape(2, -1)


def swap_qubits(stacked):
    devices = lax.axis_size("qa")
    shaped = stacked.reshape(2, devices, -1)
    moved = lax.all_to_all(shaped, "qa", split_axis=1, concat_axis=1, tiled=True)
    return moved.reshape(2, -1)


def general(state, unitaries, gate_order, gate_starts, pair_gates):
    local_bits = state.shape[1].bit_length() - 1
    global_bits = lax.axis_size("qa").bit_length() - 1
    ngates = unitaries.shape[0]
    third = ngates // 3
    stacked = state
    for k in range(third):
        stacked = dense_gate(stacked, unitaries, gate_order, gate_starts, k)
    stacked = one_qubit(stacked, pair_gates[0], local_bits - 1)
    stacked = swap_qubits(stacked)
    for k in range(third, 2 * third):
        stacked = dense_gate(stacked, unitaries, gate_order, gate_starts, k)
    stacked = one_qubit(stacked, pair_gates[1], local_bits - global_bits)
    stacked = swap_qubits(stacked)
    for k in range(2 * third, ngates):
        stacked = dense_gate(stacked, unitaries, gate_order, gate_starts, k)
    return stacked


def split(x):
    hi = x.astype(BF16)
    return hi, (x - hi.astype(F32)).astype(BF16)


def dot3(w_hi, w_lo, x):
    x_hi, x_lo = split(x)
    return jnp.dot(
        jnp.concatenate([w_hi, w_hi, w_lo], axis=1),
        jnp.concatenate([x_hi, x_lo, x_hi], axis=0),
        preferred_element_type=F32,
    )


def dot_narrow(w_hi, w_lo, x):
    n = x.shape[1]
    beside = jnp.concatenate(split(x), axis=1)
    y = jnp.dot(
        jnp.concatenate([w_hi, w_lo], axis=1),
        jnp.concatenate([beside, beside], axis=0),
        preferred_element_type=F32,
    )
    return y[:, :n] + y[:, n:]


def embed(re, im):
    return jnp.concatenate(
        [jnp.concatenate([re, -im], axis=1), jnp.concatenate([im, re], axis=1)], axis=0
    )


def my_bits():
    me = lax.axis_index("qa")
    return lax.rem(me, 2), lax.rem(lax.div(me, 2), 2)


def halves(gdim, start):
    if start == 0:
        return [pl.ds(b * gdim, gdim) for b in range(2)]
    return [pl.ds(b, gdim, stride=2) for b in range(2)]


def begin(u_re, u_im, off, flip, m):
    gdim = u_re.shape[0]
    row = lax.broadcasted_iota(jnp.int32, (gdim, 2 * gdim), 0)
    col = jnp.bitwise_xor(lax.broadcasted_iota(jnp.int32, (gdim, 2 * gdim), 1), flip)
    ones = jnp.concatenate(
        [
            jnp.where(row * (1 + off) + b * (gdim - off * (gdim - 1)) == col, 1.0, 0.0)
            for b in range(2)
        ],
        axis=1,
    ).astype(BF16)
    w_hi, w_lo = split(jnp.concatenate([u_re, u_im], axis=0))
    y = jnp.dot(
        jnp.concatenate([w_hi, w_lo], axis=1),
        jnp.concatenate([ones, ones], axis=0),
        preferred_element_type=F32,
    )
    for start in range(2):

        @pl.when(off == start)
        def _():
            store(m, [(r, j) for r in halves(gdim, start) for j in range(2)], y)


def store(m, blocks, y):
    gdim = y.shape[0] // 2
    for i, (r, j) in enumerate(blocks):
        for p in range(2):
            m[p][j, r, :] = y[p * gdim : (p + 1) * gdim, gdim * i : gdim * (i + 1)]


def apply(u_re, u_im, off, source, m):
    gdim = u_re.shape[0]
    w_hi, w_lo = split(embed(u_re, u_im))
    for start in range(2):

        @pl.when(off == start)
        def _():
            blocks = [(r, j) for r in halves(gdim, start) for j in range(2)]
            x = jnp.concatenate(
                [jnp.concatenate([v[j, r, :] for v in source], axis=0) for r, j in blocks],
                axis=1,
            )
            store(m, blocks, dot3(w_hi, w_lo, x))


def compose(count, flip, gate, m):
    begin(*gate(0), flip, m)

    def step(i, carry):
        apply(*gate(i), m, m)
        return carry

    lax.fori_loop(1, count, step, 0)


def put(ref, re, im):
    for i, w in enumerate((re, im - re, -(re + im))):
        ref[0, i], ref[1, i] = split(w)


def times(w_ref, re, im, product):
    both, t_re, t_im = (
        product(w_ref[0, i], w_ref[1, i], x) for i, x in enumerate((re + im, re, im))
    )
    return both + t_im, both + t_re


def whole(m):
    return jnp.concatenate([m[j] for j in range(2)], axis=1)


def parts_of(ref, at):
    rows = ref.shape[1] // 2
    return ref[at, pl.ds(0, rows, stride=2), :], ref[at, pl.ds(1, rows, stride=2), :]


def front_kernel(order, starts, pair, unit, w0_ref, units, flags, coef, *scratch):
    order_s, starts_s, pair_s, u, m_re, m_im, small_sems, sems, late_sems = scratch
    ngates, later = unit.shape[0], units.shape[0]
    count = ngates - later
    h0, h1 = my_bits()
    smalls = [
        pltpu.make_async_copy(a, b, small_sems.at[i])
        for i, (a, b) in enumerate(((order, order_s), (starts, starts_s), (pair, pair_s)))
    ]
    for c in smalls:
        c.start()

    def fetch(g):
        return pltpu.make_async_copy(unit.at[g], u.at[g], sems.at[g])

    def late(k):
        return pltpu.make_async_copy(unit.at[order_s[count + k]], units.at[k], late_sems.at[k])

    for g in range(ngates):
        fetch(g).start()
    for c in smalls:
        c.wait()
    for k in range(later):
        late(k).start()

    def gate(i):
        g = order_s[i]
        fetch(g).wait()
        return u[g, 0], u[g, 1], starts_s[i]

    compose(count, 0, gate, (m_re, m_im))
    put(w0_ref, whole(m_re), whole(m_im))
    bits = starts_s[count]
    for k in range(1, later):
        bits += starts_s[count + k] * 2**k
    flags[...] = jnp.full(flags.shape, bits, jnp.int32)
    for b in range(2):
        for p in range(2):
            for i, v in enumerate((pair_s[0, p, b, h1], pair_s[0, p, b, 1 - h1], pair_s[1, p, h0, b])):
                coef[i, b, p] = jnp.full(coef.shape[3:], v, F32)
    for k in range(later):
        fetch(order_s[count + k]).wait()
        late(k).wait()


def chosen(units, flags):
    bits = jnp.max(flags[...])

    def gate(k):
        return units[k, 0], units[k, 1], jnp.bitwise_and(lax.shift_right_logical(bits, k), 1)

    return gate


def second_kernel(units, flags, coef, w1_ref, re_ref, im_ref, m_re, m_im):
    count = units.shape[0] // 2
    gdim = units.shape[-1]
    half = gdim // 2
    h0, h1 = my_bits()
    gate = chosen(units, flags)
    compose(count, h1 * gdim + h0 * half, gate, (m_re, m_im))
    for k in range(2):
        at = lax.rem(h1 + k, 2) * gdim
        r, i = 0.0, 0.0
        for b in range(2):
            rows = pl.ds(pl.multiple_of(at + b * half, half), half)
            v_re, v_im = coef[2, b, 0][:1, :1], coef[2, b, 1][:1, :1]
            x_re, x_im = (
                jnp.concatenate([m[j, rows, :] for j in range(2)], axis=1) for m in (m_re, m_im)
            )
            r += v_re * x_re - v_im * x_im
            i += v_re * x_im + v_im * x_re
        w1_ref[0, k], w1_ref[1, k] = split(embed(r, i))
    compose(count // 2, 0, lambda i: gate(count + i), (re_ref, im_ref))


def third_kernel(units, flags, re, im, w_ref, m_re, m_im):
    count = units.shape[0] // 2
    gate = chosen(units, flags)
    source = (re, im)
    for k in range(count + count // 2, 2 * count):
        apply(*gate(k), source, (m_re, m_im))
        source = (m_re, m_im)
    put(w_ref, whole(source[0]), whole(source[1]))


def kept_kernel(w_ref, state, out):
    _, h1 = my_bits()
    rows, lanes = state.shape[1] // 2, state.shape[2]
    blocks = [parts_of(state, h1 * 2 + c) for c in range(2)]
    y = times(w_ref, *(jnp.concatenate(v, axis=1) for v in zip(*blocks)), dot3)
    for k in range(2):
        for p in range(2):
            out[k, p * rows : (p + 1) * rows] = y[p][:, k * lanes : (k + 1) * lanes]


def came_kernel(w_ref, raw, out):
    rows = raw.shape[1] // 2
    out[0, :rows], out[0, rows:] = times(w_ref, *parts_of(raw, 0), dot_narrow)


def through(k, chunk, w1_ref, w2_ref, kept, kept_other, mine, theirs):
    lanes = mine.shape[2]
    dim = mine.shape[1] // 2
    part = dim // 4
    sources = ((kept, chunk), (kept_other, chunk), (mine, 0), (theirs, 0))
    cols = [
        jnp.concatenate(
            [v[i, p * dim + f * part : p * dim + (f + 1) * part, :] for p in range(2) for v, i in sources],
            axis=0,
        )
        for f in range(4)
    ]
    y = dot3(w1_ref[0, k], w1_ref[1, k], jnp.concatenate(cols, axis=1))
    x = (
        jnp.concatenate(
            [y[p * part : (p + 1) * part, f * lanes : (f + 1) * lanes] for f in range(4)], axis=0
        )
        for p in range(2)
    )
    return times(w2_ref, *x, dot_narrow)


def back_kernel(chunk, *refs):
    out = refs[-1]
    dim = out.shape[1] // 2
    out[0, :dim], out[0, dim:] = through(1, chunk, *refs[:-1])


def keep_kernel(chunk, coef, *refs):
    k_re, k_im = through(0, chunk, *refs[:-2])
    dim = k_re.shape[0]
    for b, out in enumerate(refs[-2:]):
        v_re, v_im = coef[0, b, 0][:1], coef[0, b, 1][:1]
        out[0, :dim, :] = v_re * k_re - v_im * k_im
        out[0, dim:, :] = v_re * k_im + v_im * k_re


def last_kernel(chunk, part0, part1, back, coef, *refs):
    out, buf, sems = refs[-3:]
    rows = back.shape[1] // 2
    cut = rows // 2
    copies = []
    for b, part in enumerate((part0, part1)):
        for q in range(2):
            at = q * cut
            u_re, u_im = coef[1, b, 0][:1], coef[1, b, 1][:1]
            re, im = pl.ds(at, cut), pl.ds(rows + at, cut)
            b_re, b_im = back[0, re, :], back[0, im, :]
            buf[b, pl.ds(2 * at, cut, stride=2), :] = part[0, re, :] + (u_re * b_re - u_im * b_im)
            buf[b, pl.ds(2 * at + 1, cut, stride=2), :] = part[0, im, :] + (u_re * b_im + u_im * b_re)
            span = pl.ds(2 * at, 2 * cut)
            copies.append(
                pltpu.make_async_copy(
                    buf.at[b, span], out.at[b, chunk, span], sems.at[2 * b + q]
                )
            )
            copies[-1].start()
    for c in copies:
        c.wait()


VM = pl.BlockSpec(memory_space=pltpu.VMEM)
SM = pl.BlockSpec(memory_space=pltpu.SMEM)
HB = pl.BlockSpec(memory_space=pltpu.HBM)


def cost(outs, args, flops):
    nbytes = sum(a.size * a.dtype.itemsize for a in (*outs, *args))
    return pl.CostEstimate(flops=flops, bytes_accessed=nbytes, transcendentals=0)


PARAMS = pltpu.CompilerParams(vmem_limit_bytes=16 * 2**20)


def call(body, outs, args, specs, scratch=(), flops=0):
    results = pl.pallas_call(
        body,
        out_shape=outs,
        in_specs=specs,
        out_specs=[VM] * len(outs),
        scratch_shapes=scratch,
        cost_estimate=cost(outs, args, flops),
        compiler_params=PARAMS,
    )(*args)
    return list(results)


def finish(args, shape, chunk, before=None):
    args = args + ([] if before is None else [before])
    return pl.pallas_call(
        partial(last_kernel, chunk),
        out_shape=shape,
        in_specs=[VM] * 4 + [HB] * (len(args) - 4),
        out_specs=HB,
        input_output_aliases={} if before is None else {4: 0},
        scratch_shapes=[pltpu.VMEM((2, *shape.shape[2:]), F32), pltpu.SemaphoreType.DMA((4,))],
        cost_estimate=cost([shape], args[:3], 0),
        compiler_params=PARAMS,
    )(*args)


def paired(state, unitaries, gate_order, gate_starts, pair):
    devices = lax.axis_size("qa")
    count = unitaries.shape[0] // 3
    gdim = unitaries.shape[-1]
    lanes, rows, dim, half = gdim, 4 * gdim, 2 * gdim, gdim
    f32 = partial(jax.ShapeDtypeStruct, dtype=F32)
    bf16 = partial(jax.ShapeDtypeStruct, dtype=BF16)
    tie = lax.optimization_barrier
    far = partial(pltpu.with_memory_space_constraint, memory_space=pltpu.HBM)
    _, h1 = my_bits()

    def other(v, bit):
        return lax.ppermute(v, "qa", [(i, i ^ bit) for i in range(devices)])

    def block_of(v, c):
        return lax.dynamic_slice_in_dim(v, (1 - h1) * 2 + c, 1, axis=0)

    view = state.reshape(2, -1, lanes).transpose(1, 0, 2).reshape(4, rows, lanes)
    came = [other(block_of(view, c), 2) for c in range(2)]
    step = 3 * 2 * (2 * gdim) * (2 * gdim) * (4 * gdim)
    enter_flops = 6 * rows * rows * lanes
    block, both = f32((1, rows, lanes)), f32((2, rows, lanes))
    m = f32((2, dim, gdim))
    m_scratch = pltpu.VMEM(m.shape, F32)
    small = [gate_order, gate_starts, pair]
    ngates = unitaries.shape[0]
    tile = (8, lanes)
    dma = pltpu.SemaphoreType.DMA
    w0, units, flags, coef = call(
        front_kernel,
        [
            bf16((2, 3, dim, dim)),
            f32((2 * count, *unitaries.shape[1:])),
            jax.ShapeDtypeStruct(tile, jnp.int32),
            f32((3, 2, 2, *tile)),
        ],
        [far(v) for v in (*small, unitaries)],
        [HB] * 4,
        [pltpu.SMEM(v.shape, v.dtype) for v in small]
        + [pltpu.VMEM(unitaries.shape, F32), m_scratch, m_scratch]
        + [dma((3,)), dma((ngates,)), dma((2 * count,))],
        flops=count * step,
    )
    w1, re2, im2 = call(
        second_kernel,
        [bf16((2, 2, half, rows)), m, m],
        [units, flags, coef],
        [VM] * 3,
        [m_scratch, m_scratch],
        flops=3 * count * step // 2,
    )
    (kept,) = call(kept_kernel, [both], [w0, view], [VM] * 2, flops=2 * enter_flops)
    kept_other = other(kept, 1)
    re2, kept = tie((re2, kept))
    came[0], re2 = tie((came[0], re2))
    (mine,) = call(came_kernel, [block], [w0, came[0]], [VM] * 2, flops=enter_flops)
    re2, mine = tie((re2, mine))
    (w2,) = call(
        third_kernel,
        [bf16((2, 3, dim, dim))],
        [units, flags, re2, im2],
        [VM] * 4,
        [m_scratch, m_scratch],
        flops=count * step // 2,
    )

    def rest(c, mine):
        theirs = other(mine, 1)
        blocks = [w1, w2, kept, kept_other, mine, theirs]
        (back,) = call(partial(back_kernel, c), [block], blocks, [VM] * 6, flops=2 * enter_flops)
        return blocks, other(back, 2)

    def keep(c, blocks):
        return call(
            partial(keep_kernel, c),
            [block, block],
            [coef, *blocks],
            [VM] * 7,
            flops=2 * enter_flops,
        )

    shape = f32((2, 2, rows, lanes))
    blocks0, back0 = rest(0, mine)
    (mine,) = call(came_kernel, [block], [w0, came[1]], [VM] * 2, flops=enter_flops)
    blocks1, back1 = rest(1, mine)
    blocks0[0], blocks1[4] = tie((blocks0[0], blocks1[4]))
    keep0 = keep(0, blocks0)
    keep1 = keep(1, blocks1)
    back0, keep1[0] = tie((back0, keep1[0]))
    out = finish([*keep0, back0, coef], shape, 0)
    out = finish([*keep1, back1, coef], shape, 1, out)
    return out.reshape(-1, 2, lanes).transpose(1, 0, 2).reshape(2, -1)


def meets_two(state, unitaries, devices):
    local_bits = state.shape[1].bit_length() - 1
    global_bits = devices.bit_length() - 1
    top = 2 * (unitaries.shape[-1].bit_length() - 1) + 1
    met = top - (local_bits - global_bits)
    return met == 2 and local_bits == top + 2 and global_bits >= 2


def shards(*args):
    if meets_two(args[0], args[1], lax.axis_size("qa")):
        return paired(*args)
    return general(*args)


def solution(mesh):
    placed = (P(None, ("cuts", "qa")), P(), P(), P(), P())
    return jax.shard_map(
        shards, mesh=mesh, in_specs=placed, out_specs=P(None, ("cuts", "qa")), check_vma=False
    )
```

```python
from functools import partial

import jax
import jax.numpy as jnp
from jax import lax
from jax.experimental import pallas as pl
from jax.experimental.pallas import tpu as pltpu
from jax.sharding import PartitionSpec as P


HIGH = lax.Precision.HIGHEST
F32 = jnp.float32
BF16 = jnp.bfloat16


def mix(mat, vec):
    return jnp.einsum("ij,ajb->aib", mat, vec, precision=HIGH)


def dense_branch(re_part, im_part, u_re, u_im, offset):
    gdim = u_re.shape[0]
    gq = gdim.bit_length() - 1
    block = 2 ** (gq + offset)
    shaped_re = re_part.reshape(-1, gdim, block)
    shaped_im = im_part.reshape(-1, gdim, block)
    new_re = mix(u_re, shaped_re) - mix(u_im, shaped_im)
    new_im = mix(u_re, shaped_im) + mix(u_im, shaped_re)
    return (new_re.reshape(-1), new_im.reshape(-1))


def dense_gate(stacked, unitaries, gate_order, gate_starts, k):
    chosen = unitaries[gate_order[k]]
    branches = [partial(dense_branch, offset=0), partial(dense_branch, offset=1)]
    new_re, new_im = lax.switch(
        gate_starts[k], branches, stacked[0], stacked[1], chosen[0], chosen[1]
    )
    return jnp.stack([new_re, new_im])


def one_qubit(stacked, gate, qubit):
    shaped = stacked.reshape(2, -1, 2, 2**qubit)
    u_re, u_im = (gate[0], gate[1])
    new_re = jnp.einsum("bc,acx->abx", u_re, shaped[0], precision=HIGH) - jnp.einsum(
        "bc,acx->abx", u_im, shaped[1], precision=HIGH
    )
    new_im = jnp.einsum("bc,acx->abx", u_re, shaped[1], precision=HIGH) + jnp.einsum(
        "bc,acx->abx", u_im, shaped[0], precision=HIGH
    )
    return jnp.stack([new_re, new_im]).reshape(2, -1)


def swap_qubits(stacked):
    devices = lax.axis_size("qa")
    shaped = stacked.reshape(2, devices, -1)
    moved = lax.all_to_all(shaped, "qa", split_axis=1, concat_axis=1, tiled=True)
    return moved.reshape(2, -1)


def general(state, unitaries, gate_order, gate_starts, pair_gates):
    local_bits = state.shape[1].bit_length() - 1
    global_bits = lax.axis_size("qa").bit_length() - 1
    ngates = unitaries.shape[0]
    third = ngates // 3
    stacked = state
    for k in range(third):
        stacked = dense_gate(stacked, unitaries, gate_order, gate_starts, k)
    stacked = one_qubit(stacked, pair_gates[0], local_bits - 1)
    stacked = swap_qubits(stacked)
    for k in range(third, 2 * third):
        stacked = dense_gate(stacked, unitaries, gate_order, gate_starts, k)
    stacked = one_qubit(stacked, pair_gates[1], local_bits - global_bits)
    stacked = swap_qubits(stacked)
    for k in range(2 * third, ngates):
        stacked = dense_gate(stacked, unitaries, gate_order, gate_starts, k)
    return stacked


def split(x):
    hi = x.astype(BF16)
    return hi, (x - hi.astype(F32)).astype(BF16)


def dot3(w_hi, w_lo, x):
    x_hi, x_lo = split(x)
    return jnp.dot(
        jnp.concatenate([w_hi, w_hi, w_lo], axis=1),
        jnp.concatenate([x_hi, x_lo, x_hi], axis=0),
        preferred_element_type=F32,
    )


def dot_narrow(w_hi, w_lo, x):
    n = x.shape[1]
    beside = jnp.concatenate(split(x), axis=1)
    y = jnp.dot(
        jnp.concatenate([w_hi, w_lo], axis=1),
        jnp.concatenate([beside, beside], axis=0),
        preferred_element_type=F32,
    )
    return y[:, :n] + y[:, n:]


def embed(re, im):
    return jnp.concatenate(
        [jnp.concatenate([re, -im], axis=1), jnp.concatenate([im, re], axis=1)], axis=0
    )


def my_bits():
    me = lax.axis_index("qa")
    return lax.rem(me, 2), lax.rem(lax.div(me, 2), 2)


def halves(gdim, start):
    if start == 0:
        return [pl.ds(b * gdim, gdim) for b in range(2)]
    return [pl.ds(b, gdim, stride=2) for b in range(2)]


def begin(u_re, u_im, off, flip, m):
    gdim = u_re.shape[0]
    row = lax.broadcasted_iota(jnp.int32, (gdim, 2 * gdim), 0)
    col = jnp.bitwise_xor(lax.broadcasted_iota(jnp.int32, (gdim, 2 * gdim), 1), flip)
    ones = jnp.concatenate(
        [
            jnp.where(row * (1 + off) + b * (gdim - off * (gdim - 1)) == col, 1.0, 0.0)
            for b in range(2)
        ],
        axis=1,
    ).astype(BF16)
    w_hi, w_lo = split(jnp.concatenate([u_re, u_im], axis=0))
    y = jnp.dot(
        jnp.concatenate([w_hi, w_lo], axis=1),
        jnp.concatenate([ones, ones], axis=0),
        preferred_element_type=F32,
    )
    for start in range(2):

        @pl.when(off == start)
        def _():
            store(m, [(r, j) for r in halves(gdim, start) for j in range(2)], y)


def store(m, blocks, y):
    gdim = y.shape[0] // 2
    for i, (r, j) in enumerate(blocks):
        for p in range(2):
            m[p][j, r, :] = y[p * gdim : (p + 1) * gdim, gdim * i : gdim * (i + 1)]


def apply(u_re, u_im, off, source, m):
    gdim = u_re.shape[0]
    w_hi, w_lo = split(embed(u_re, u_im))
    for start in range(2):

        @pl.when(off == start)
        def _():
            blocks = [(r, j) for r in halves(gdim, start) for j in range(2)]
            x = jnp.concatenate(
                [jnp.concatenate([v[j, r, :] for v in source], axis=0) for r, j in blocks],
                axis=1,
            )
            store(m, blocks, dot3(w_hi, w_lo, x))


def compose(count, flip, gate, m):
    begin(*gate(0), flip, m)

    def step(i, carry):
        apply(*gate(i), m, m)
        return carry

    lax.fori_loop(1, count, step, 0)


def put(ref, re, im):
    for i, w in enumerate((re, im - re, -(re + im))):
        ref[0, i], ref[1, i] = split(w)


def times(w_ref, re, im, product):
    both, t_re, t_im = (
        product(w_ref[0, i], w_ref[1, i], x) for i, x in enumerate((re + im, re, im))
    )
    return both + t_im, both + t_re


def whole(m):
    return jnp.concatenate([m[j] for j in range(2)], axis=1)


def parts_of(ref, at):
    rows = ref.shape[1] // 2
    return ref[at, pl.ds(0, rows, stride=2), :], ref[at, pl.ds(1, rows, stride=2), :]


def front_kernel(order, starts, pair, unit, w0_ref, units, flags, coef, *scratch):
    order_s, starts_s, pair_s, u, m_re, m_im, small_sems, sems, late_sems = scratch
    ngates, later = unit.shape[0], units.shape[0]
    count = ngates - later
    h0, h1 = my_bits()
    smalls = [
        pltpu.make_async_copy(a, b, small_sems.at[i])
        for i, (a, b) in enumerate(((order, order_s), (starts, starts_s), (pair, pair_s)))
    ]
    for c in smalls:
        c.start()

    def fetch(g):
        return pltpu.make_async_copy(unit.at[g], u.at[g], sems.at[g])

    def late(k):
        return pltpu.make_async_copy(unit.at[order_s[count + k]], units.at[k], late_sems.at[k])

    for g in range(ngates):
        fetch(g).start()
    for c in smalls:
        c.wait()
    for k in range(later):
        late(k).start()

    def gate(i):
        g = order_s[i]
        fetch(g).wait()
        return u[g, 0], u[g, 1], starts_s[i]

    compose(count, 0, gate, (m_re, m_im))
    put(w0_ref, whole(m_re), whole(m_im))
    bits = starts_s[count]
    for k in range(1, later):
        bits += starts_s[count + k] * 2**k
    flags[...] = jnp.full(flags.shape, bits, jnp.int32)
    for b in range(2):
        for p in range(2):
            for i, v in enumerate((pair_s[0, p, b, h1], pair_s[0, p, b, 1 - h1], pair_s[1, p, h0, b])):
                coef[i, b, p] = jnp.full(coef.shape[3:], v, F32)
    for k in range(later):
        fetch(order_s[count + k]).wait()
        late(k).wait()


def chosen(units, flags):
    bits = jnp.max(flags[...])

    def gate(k):
        return units[k, 0], units[k, 1], jnp.bitwise_and(lax.shift_right_logical(bits, k), 1)

    return gate


def second_kernel(units, flags, re, im):
    gdim = units.shape[-1]
    h0, h1 = my_bits()
    compose(units.shape[0] // 2, h1 * gdim + h0 * (gdim // 2), chosen(units, flags), (re, im))


def half_kernel(units, flags, coef, m_re, m_im, w1_ref, re_ref, im_ref):
    count = units.shape[0] // 2
    gdim = units.shape[-1]
    half = gdim // 2
    _, h1 = my_bits()
    gate = chosen(units, flags)
    for k in range(2):
        at = lax.rem(h1 + k, 2) * gdim
        r, i = 0.0, 0.0
        for b in range(2):
            rows = pl.ds(pl.multiple_of(at + b * half, half), half)
            v_re, v_im = coef[2, b, 0][:1, :1], coef[2, b, 1][:1, :1]
            x_re, x_im = (
                jnp.concatenate([m[j, rows, :] for j in range(2)], axis=1) for m in (m_re, m_im)
            )
            r += v_re * x_re - v_im * x_im
            i += v_re * x_im + v_im * x_re
        w1_ref[0, k], w1_ref[1, k] = split(embed(r, i))
    compose(count // 2, 0, lambda i: gate(count + i), (re_ref, im_ref))


def third_kernel(units, flags, re, im, w_ref, m_re, m_im):
    count = units.shape[0] // 2
    gate = chosen(units, flags)
    source = (re, im)
    for k in range(count + count // 2, 2 * count):
        apply(*gate(k), source, (m_re, m_im))
        source = (m_re, m_im)
    put(w_ref, whole(source[0]), whole(source[1]))


def kept_kernel(w_ref, state, out):
    _, h1 = my_bits()
    rows, lanes = state.shape[1] // 2, state.shape[2]
    blocks = [parts_of(state, h1 * 2 + c) for c in range(2)]
    y = times(w_ref, *(jnp.concatenate(v, axis=1) for v in zip(*blocks)), dot3)
    for k in range(2):
        for p in range(2):
            out[k, p * rows : (p + 1) * rows] = y[p][:, k * lanes : (k + 1) * lanes]


def came_kernel(w_ref, raw, out):
    rows = raw.shape[1] // 2
    out[0, :rows], out[0, rows:] = times(w_ref, *parts_of(raw, 0), dot_narrow)


def through(k, chunk, w1_ref, w2_ref, kept, kept_other, mine, theirs):
    lanes = mine.shape[2]
    dim = mine.shape[1] // 2
    part = dim // 4
    sources = ((kept, chunk), (kept_other, chunk), (mine, 0), (theirs, 0))
    cols = [
        jnp.concatenate(
            [v[i, p * dim + f * part : p * dim + (f + 1) * part, :] for p in range(2) for v, i in sources],
            axis=0,
        )
        for f in range(4)
    ]
    y = dot3(w1_ref[0, k], w1_ref[1, k], jnp.concatenate(cols, axis=1))
    x = (
        jnp.concatenate(
            [y[p * part : (p + 1) * part, f * lanes : (f + 1) * lanes] for f in range(4)], axis=0
        )
        for p in range(2)
    )
    return times(w2_ref, *x, dot_narrow)


def back_kernel(chunk, *refs):
    out = refs[-1]
    dim = out.shape[1] // 2
    out[0, :dim], out[0, dim:] = through(1, chunk, *refs[:-1])


def keep_kernel(chunk, coef, *refs):
    k_re, k_im = through(0, chunk, *refs[:-2])
    dim = k_re.shape[0]
    for b, out in enumerate(refs[-2:]):
        v_re, v_im = coef[0, b, 0][:1], coef[0, b, 1][:1]
        out[0, :dim, :] = v_re * k_re - v_im * k_im
        out[0, dim:, :] = v_re * k_im + v_im * k_re


def last_kernel(chunk, part0, part1, back, coef, *refs):
    out, buf, sems = refs[-3:]
    rows = back.shape[1] // 2
    cut = rows // 2
    copies = []
    for b, part in enumerate((part0, part1)):
        for q in range(2):
            at = q * cut
            u_re, u_im = coef[1, b, 0][:1], coef[1, b, 1][:1]
            re, im = pl.ds(at, cut), pl.ds(rows + at, cut)
            b_re, b_im = back[0, re, :], back[0, im, :]
            buf[b, pl.ds(2 * at, cut, stride=2), :] = part[0, re, :] + (u_re * b_re - u_im * b_im)
            buf[b, pl.ds(2 * at + 1, cut, stride=2), :] = part[0, im, :] + (u_re * b_im + u_im * b_re)
            span = pl.ds(2 * at, 2 * cut)
            copies.append(
                pltpu.make_async_copy(
                    buf.at[b, span], out.at[b, chunk, span], sems.at[2 * b + q]
                )
            )
            copies[-1].start()
    for c in copies:
        c.wait()


VM = pl.BlockSpec(memory_space=pltpu.VMEM)
SM = pl.BlockSpec(memory_space=pltpu.SMEM)
HB = pl.BlockSpec(memory_space=pltpu.HBM)


def cost(outs, args, flops):
    nbytes = sum(a.size * a.dtype.itemsize for a in (*outs, *args))
    return pl.CostEstimate(flops=flops, bytes_accessed=nbytes, transcendentals=0)


PARAMS = pltpu.CompilerParams(vmem_limit_bytes=16 * 2**20)


def call(body, outs, args, specs, scratch=(), flops=0):
    results = pl.pallas_call(
        body,
        out_shape=outs,
        in_specs=specs,
        out_specs=[VM] * len(outs),
        scratch_shapes=scratch,
        cost_estimate=cost(outs, args, flops),
        compiler_params=PARAMS,
    )(*args)
    return list(results)


def finish(args, shape, chunk, before=None):
    args = args + ([] if before is None else [before])
    return pl.pallas_call(
        partial(last_kernel, chunk),
        out_shape=shape,
        in_specs=[VM] * 4 + [HB] * (len(args) - 4),
        out_specs=HB,
        input_output_aliases={} if before is None else {4: 0},
        scratch_shapes=[pltpu.VMEM((2, *shape.shape[2:]), F32), pltpu.SemaphoreType.DMA((4,))],
        cost_estimate=cost([shape], args[:3], 0),
        compiler_params=PARAMS,
    )(*args)


def paired(state, unitaries, gate_order, gate_starts, pair):
    devices = lax.axis_size("qa")
    count = unitaries.shape[0] // 3
    gdim = unitaries.shape[-1]
    lanes, rows, dim, half = gdim, 4 * gdim, 2 * gdim, gdim
    f32 = partial(jax.ShapeDtypeStruct, dtype=F32)
    bf16 = partial(jax.ShapeDtypeStruct, dtype=BF16)
    tie = lax.optimization_barrier
    far = partial(pltpu.with_memory_space_constraint, memory_space=pltpu.HBM)
    _, h1 = my_bits()

    def other(v, bit):
        return lax.ppermute(v, "qa", [(i, i ^ bit) for i in range(devices)])

    def block_of(v, c):
        return lax.dynamic_slice_in_dim(v, (1 - h1) * 2 + c, 1, axis=0)

    view = state.reshape(2, -1, lanes).transpose(1, 0, 2).reshape(4, rows, lanes)
    came = [other(block_of(view, c), 2) for c in range(2)]
    step = 3 * 2 * (2 * gdim) * (2 * gdim) * (4 * gdim)
    enter_flops = 6 * rows * rows * lanes
    block, both = f32((1, rows, lanes)), f32((2, rows, lanes))
    m = f32((2, dim, gdim))
    m_scratch = pltpu.VMEM(m.shape, F32)
    small = [gate_order, gate_starts, pair]
    ngates = unitaries.shape[0]
    tile = (8, lanes)
    dma = pltpu.SemaphoreType.DMA
    w0, units, flags, coef = call(
        front_kernel,
        [
            bf16((2, 3, dim, dim)),
            f32((2 * count, *unitaries.shape[1:])),
            jax.ShapeDtypeStruct(tile, jnp.int32),
            f32((3, 2, 2, *tile)),
        ],
        [far(v) for v in (*small, unitaries)],
        [HB] * 4,
        [pltpu.SMEM(v.shape, v.dtype) for v in small]
        + [pltpu.VMEM(unitaries.shape, F32), m_scratch, m_scratch]
        + [dma((3,)), dma((ngates,)), dma((2 * count,))],
        flops=count * step,
    )
    re1, im1 = call(second_kernel, [m, m], [units, flags], [VM] * 2, flops=count * step)
    w0, re1 = tie((w0, re1))
    (kept,) = call(kept_kernel, [both], [w0, view], [VM] * 2, flops=2 * enter_flops)
    kept_other = other(kept, 1)
    units, kept = tie((units, kept))
    w1, re2, im2 = call(
        half_kernel,
        [bf16((2, 2, half, rows)), m, m],
        [units, flags, coef, re1, im1],
        [VM] * 5,
        flops=count * step // 2,
    )
    came[0], re2 = tie((came[0], re2))
    (mine,) = call(came_kernel, [block], [w0, came[0]], [VM] * 2, flops=enter_flops)
    re2, mine = tie((re2, mine))
    (w2,) = call(
        third_kernel,
        [bf16((2, 3, dim, dim))],
        [units, flags, re2, im2],
        [VM] * 4,
        [m_scratch, m_scratch],
        flops=count * step // 2,
    )

    def rest(c, mine):
        theirs = other(mine, 1)
        blocks = [w1, w2, kept, kept_other, mine, theirs]
        (back,) = call(partial(back_kernel, c), [block], blocks, [VM] * 6, flops=2 * enter_flops)
        return blocks, other(back, 2)

    def keep(c, blocks):
        return call(
            partial(keep_kernel, c),
            [block, block],
            [coef, *blocks],
            [VM] * 7,
            flops=2 * enter_flops,
        )

    shape = f32((2, 2, rows, lanes))
    blocks0, back0 = rest(0, mine)
    (mine,) = call(came_kernel, [block], [w0, came[1]], [VM] * 2, flops=enter_flops)
    blocks1, back1 = rest(1, mine)
    blocks0[0], blocks1[4] = tie((blocks0[0], blocks1[4]))
    keep0 = keep(0, blocks0)
    keep1 = keep(1, blocks1)
    back0, keep1[0] = tie((back0, keep1[0]))
    out = finish([*keep0, back0, coef], shape, 0)
    out = finish([*keep1, back1, coef], shape, 1, out)
    return out.reshape(-1, 2, lanes).transpose(1, 0, 2).reshape(2, -1)


def meets_two(state, unitaries, devices):
    local_bits = state.shape[1].bit_length() - 1
    global_bits = devices.bit_length() - 1
    top = 2 * (unitaries.shape[-1].bit_length() - 1) + 1
    met = top - (local_bits - global_bits)
    return met == 2 and local_bits == top + 2 and global_bits >= 2


def shards(*args):
    if meets_two(args[0], args[1], lax.axis_size("qa")):
        return paired(*args)
    return general(*args)


def solution(mesh):
    placed = (P(None, ("cuts", "qa")), P(), P(), P(), P())
    return jax.shard_map(
        shards, mesh=mesh, in_specs=placed, out_specs=P(None, ("cuts", "qa")), check_vma=False
    )
```

```python
from functools import partial

import jax
import jax.numpy as jnp
from jax import lax
from jax.experimental import pallas as pl
from jax.experimental.pallas import tpu as pltpu
from jax.sharding import PartitionSpec as P


HIGH = lax.Precision.HIGHEST
F32 = jnp.float32
BF16 = jnp.bfloat16


def mix(mat, vec):
    return jnp.einsum("ij,ajb->aib", mat, vec, precision=HIGH)


def dense_branch(re_part, im_part, u_re, u_im, offset):
    gdim = u_re.shape[0]
    gq = gdim.bit_length() - 1
    block = 2 ** (gq + offset)
    shaped_re = re_part.reshape(-1, gdim, block)
    shaped_im = im_part.reshape(-1, gdim, block)
    new_re = mix(u_re, shaped_re) - mix(u_im, shaped_im)
    new_im = mix(u_re, shaped_im) + mix(u_im, shaped_re)
    return (new_re.reshape(-1), new_im.reshape(-1))


def dense_gate(stacked, unitaries, gate_order, gate_starts, k):
    chosen = unitaries[gate_order[k]]
    branches = [partial(dense_branch, offset=0), partial(dense_branch, offset=1)]
    new_re, new_im = lax.switch(
        gate_starts[k], branches, stacked[0], stacked[1], chosen[0], chosen[1]
    )
    return jnp.stack([new_re, new_im])


def one_qubit(stacked, gate, qubit):
    shaped = stacked.reshape(2, -1, 2, 2**qubit)
    u_re, u_im = (gate[0], gate[1])
    new_re = jnp.einsum("bc,acx->abx", u_re, shaped[0], precision=HIGH) - jnp.einsum(
        "bc,acx->abx", u_im, shaped[1], precision=HIGH
    )
    new_im = jnp.einsum("bc,acx->abx", u_re, shaped[1], precision=HIGH) + jnp.einsum(
        "bc,acx->abx", u_im, shaped[0], precision=HIGH
    )
    return jnp.stack([new_re, new_im]).reshape(2, -1)


def swap_qubits(stacked):
    devices = lax.axis_size("qa")
    shaped = stacked.reshape(2, devices, -1)
    moved = lax.all_to_all(shaped, "qa", split_axis=1, concat_axis=1, tiled=True)
    return moved.reshape(2, -1)


def general(state, unitaries, gate_order, gate_starts, pair_gates):
    local_bits = state.shape[1].bit_length() - 1
    global_bits = lax.axis_size("qa").bit_length() - 1
    ngates = unitaries.shape[0]
    third = ngates // 3
    stacked = state
    for k in range(third):
        stacked = dense_gate(stacked, unitaries, gate_order, gate_starts, k)
    stacked = one_qubit(stacked, pair_gates[0], local_bits - 1)
    stacked = swap_qubits(stacked)
    for k in range(third, 2 * third):
        stacked = dense_gate(stacked, unitaries, gate_order, gate_starts, k)
    stacked = one_qubit(stacked, pair_gates[1], local_bits - global_bits)
    stacked = swap_qubits(stacked)
    for k in range(2 * third, ngates):
        stacked = dense_gate(stacked, unitaries, gate_order, gate_starts, k)
    return stacked


def split(x):
    hi = x.astype(BF16)
    return hi, (x - hi.astype(F32)).astype(BF16)


def dot3(w_hi, w_lo, x):
    x_hi, x_lo = split(x)
    return jnp.dot(
        jnp.concatenate([w_hi, w_hi, w_lo], axis=1),
        jnp.concatenate([x_hi, x_lo, x_hi], axis=0),
        preferred_element_type=F32,
    )


def dot_narrow(w_hi, w_lo, x):
    n = x.shape[1]
    beside = jnp.concatenate(split(x), axis=1)
    y = jnp.dot(
        jnp.concatenate([w_hi, w_lo], axis=1),
        jnp.concatenate([beside, beside], axis=0),
        preferred_element_type=F32,
    )
    return y[:, :n] + y[:, n:]


def embed(re, im):
    return jnp.concatenate(
        [jnp.concatenate([re, -im], axis=1), jnp.concatenate([im, re], axis=1)], axis=0
    )


def my_bits():
    me = lax.axis_index("qa")
    return lax.rem(me, 2), lax.rem(lax.div(me, 2), 2)


def halves(gdim, start):
    if start == 0:
        return [pl.ds(b * gdim, gdim) for b in range(2)]
    return [pl.ds(b, gdim, stride=2) for b in range(2)]


def begin(u_re, u_im, off, flip, m):
    gdim = u_re.shape[0]
    row = lax.broadcasted_iota(jnp.int32, (gdim, 2 * gdim), 0)
    col = jnp.bitwise_xor(lax.broadcasted_iota(jnp.int32, (gdim, 2 * gdim), 1), flip)
    ones = jnp.concatenate(
        [
            jnp.where(row * (1 + off) + b * (gdim - off * (gdim - 1)) == col, 1.0, 0.0)
            for b in range(2)
        ],
        axis=1,
    ).astype(BF16)
    w_hi, w_lo = split(jnp.concatenate([u_re, u_im], axis=0))
    y = jnp.dot(
        jnp.concatenate([w_hi, w_lo], axis=1),
        jnp.concatenate([ones, ones], axis=0),
        preferred_element_type=F32,
    )
    for start in range(2):

        @pl.when(off == start)
        def _():
            store(m, [(r, j) for r in halves(gdim, start) for j in range(2)], y)


def store(m, blocks, y):
    gdim = y.shape[0] // 2
    for i, (r, j) in enumerate(blocks):
        for p in range(2):
            m[p][j, r, :] = y[p * gdim : (p + 1) * gdim, gdim * i : gdim * (i + 1)]


def apply(u_re, u_im, off, source, m):
    gdim = u_re.shape[0]
    w_hi, w_lo = split(embed(u_re, u_im))
    for start in range(2):

        @pl.when(off == start)
        def _():
            blocks = [(r, j) for r in halves(gdim, start) for j in range(2)]
            x = jnp.concatenate(
                [jnp.concatenate([v[j, r, :] for v in source], axis=0) for r, j in blocks],
                axis=1,
            )
            store(m, blocks, dot3(w_hi, w_lo, x))


def compose(count, flip, gate, m):
    begin(*gate(0), flip, m)

    def step(i, carry):
        apply(*gate(i), m, m)
        return carry

    lax.fori_loop(1, count, step, 0)


def put(ref, re, im):
    for i, w in enumerate((re, im - re, -(re + im))):
        ref[0, i], ref[1, i] = split(w)


def times(w_ref, re, im, product):
    both, t_re, t_im = (
        product(w_ref[0, i], w_ref[1, i], x) for i, x in enumerate((re + im, re, im))
    )
    return both + t_im, both + t_re


def whole(m):
    return jnp.concatenate([m[j] for j in range(2)], axis=1)


def parts_of(ref, at):
    rows = ref.shape[1] // 2
    return ref[at, pl.ds(0, rows, stride=2), :], ref[at, pl.ds(1, rows, stride=2), :]


def front_kernel(order, starts, pair, unit, w0_ref, w1_ref, units, flags, coef, *scratch):
    order_s, starts_s, pair_s, u, m_re, m_im, small_sems, sems, late_sems = scratch
    ngates, later, gdim = unit.shape[0], units.shape[0], unit.shape[-1]
    count, half = ngates - later, gdim // 2
    h0, h1 = my_bits()
    smalls = [
        pltpu.make_async_copy(a, b, small_sems.at[i])
        for i, (a, b) in enumerate(((order, order_s), (starts, starts_s), (pair, pair_s)))
    ]
    for c in smalls:
        c.start()

    def fetch(g):
        return pltpu.make_async_copy(unit.at[g], u.at[g], sems.at[g])

    def late(k):
        return pltpu.make_async_copy(unit.at[order_s[count + k]], units.at[k], late_sems.at[k])

    for g in range(ngates):
        fetch(g).start()
    for c in smalls:
        c.wait()
    for k in range(later):
        late(k).start()

    def gate(i):
        g = order_s[i]
        fetch(g).wait()
        return u[g, 0], u[g, 1], starts_s[i]

    compose(later, 0, gate, (m_re, m_im))
    put(w0_ref, whole(m_re), whole(m_im))
    compose(later, h1 * gdim + h0 * half, lambda i: gate(later + i), (m_re, m_im))
    for k in range(2):
        at = lax.rem(h1 + k, 2) * gdim
        r, i = 0.0, 0.0
        for b in range(2):
            rows = pl.ds(pl.multiple_of(at + b * half, half), half)
            v_re, v_im = pair_s[1, 0, h0, b], pair_s[1, 1, h0, b]
            x_re, x_im = (
                jnp.concatenate([m[j, rows, :] for j in range(2)], axis=1) for m in (m_re, m_im)
            )
            r += v_re * x_re - v_im * x_im
            i += v_re * x_im + v_im * x_re
        w1_ref[0, k], w1_ref[1, k] = split(embed(r, i))
    bits = starts_s[count]
    for k in range(1, later):
        bits += starts_s[count + k] * 2**k
    flags[...] = jnp.full(flags.shape, bits, jnp.int32)
    for b in range(2):
        for p in range(2):
            for i, v in enumerate((pair_s[0, p, b, h1], pair_s[0, p, b, 1 - h1])):
                coef[i, b, p] = jnp.full(coef.shape[3:], v, F32)
    for k in range(later):
        fetch(order_s[count + k]).wait()
        late(k).wait()


def chosen(units, flags):
    bits = jnp.max(flags[...])

    def gate(k):
        return units[k, 0], units[k, 1], jnp.bitwise_and(lax.shift_right_logical(bits, k), 1)

    return gate


def half_kernel(units, flags, re, im):
    compose(units.shape[0] // 2, 0, chosen(units, flags), (re, im))


def third_kernel(units, flags, re, im, w_ref, m_re, m_im):
    count = units.shape[0]
    gate = chosen(units, flags)
    source = (re, im)
    for k in range(count // 2, count):
        apply(*gate(k), source, (m_re, m_im))
        source = (m_re, m_im)
    put(w_ref, whole(source[0]), whole(source[1]))


def kept_kernel(w_ref, state, out):
    _, h1 = my_bits()
    rows, lanes = state.shape[1] // 2, state.shape[2]
    blocks = [parts_of(state, h1 * 2 + c) for c in range(2)]
    y = times(w_ref, *(jnp.concatenate(v, axis=1) for v in zip(*blocks)), dot3)
    for k in range(2):
        for p in range(2):
            out[k, p * rows : (p + 1) * rows] = y[p][:, k * lanes : (k + 1) * lanes]


def came_kernel(w_ref, raw, out):
    rows = raw.shape[1] // 2
    out[0, :rows], out[0, rows:] = times(w_ref, *parts_of(raw, 0), dot_narrow)


def through(k, chunk, w1_ref, w2_ref, kept, kept_other, mine, theirs):
    lanes = mine.shape[2]
    dim = mine.shape[1] // 2
    part = dim // 4
    sources = ((kept, chunk), (kept_other, chunk), (mine, 0), (theirs, 0))
    cols = [
        jnp.concatenate(
            [v[i, p * dim + f * part : p * dim + (f + 1) * part, :] for p in range(2) for v, i in sources],
            axis=0,
        )
        for f in range(4)
    ]
    y = dot3(w1_ref[0, k], w1_ref[1, k], jnp.concatenate(cols, axis=1))
    x = (
        jnp.concatenate(
            [y[p * part : (p + 1) * part, f * lanes : (f + 1) * lanes] for f in range(4)], axis=0
        )
        for p in range(2)
    )
    return times(w2_ref, *x, dot_narrow)


def back_kernel(chunk, *refs):
    out = refs[-1]
    dim = out.shape[1] // 2
    out[0, :dim], out[0, dim:] = through(1, chunk, *refs[:-1])


def keep_kernel(chunk, coef, *refs):
    k_re, k_im = through(0, chunk, *refs[:-2])
    dim = k_re.shape[0]
    for b, out in enumerate(refs[-2:]):
        v_re, v_im = coef[0, b, 0][:1], coef[0, b, 1][:1]
        out[0, :dim, :] = v_re * k_re - v_im * k_im
        out[0, dim:, :] = v_re * k_im + v_im * k_re


def last_kernel(chunk, part0, part1, back, coef, *refs):
    out, buf, sems = refs[-3:]
    rows = back.shape[1] // 2
    cut = rows // 2
    copies = []
    for b, part in enumerate((part0, part1)):
        for q in range(2):
            at = q * cut
            u_re, u_im = coef[1, b, 0][:1], coef[1, b, 1][:1]
            re, im = pl.ds(at, cut), pl.ds(rows + at, cut)
            b_re, b_im = back[0, re, :], back[0, im, :]
            buf[b, pl.ds(2 * at, cut, stride=2), :] = part[0, re, :] + (u_re * b_re - u_im * b_im)
            buf[b, pl.ds(2 * at + 1, cut, stride=2), :] = part[0, im, :] + (u_re * b_im + u_im * b_re)
            span = pl.ds(2 * at, 2 * cut)
            copies.append(
                pltpu.make_async_copy(
                    buf.at[b, span], out.at[b, chunk, span], sems.at[2 * b + q]
                )
            )
            copies[-1].start()
    for c in copies:
        c.wait()


VM = pl.BlockSpec(memory_space=pltpu.VMEM)
SM = pl.BlockSpec(memory_space=pltpu.SMEM)
HB = pl.BlockSpec(memory_space=pltpu.HBM)


def cost(outs, args, flops):
    nbytes = sum(a.size * a.dtype.itemsize for a in (*outs, *args))
    return pl.CostEstimate(flops=flops, bytes_accessed=nbytes, transcendentals=0)


PARAMS = pltpu.CompilerParams(vmem_limit_bytes=16 * 2**20)


def call(body, outs, args, specs, scratch=(), flops=0):
    results = pl.pallas_call(
        body,
        out_shape=outs,
        in_specs=specs,
        out_specs=[VM] * len(outs),
        scratch_shapes=scratch,
        cost_estimate=cost(outs, args, flops),
        compiler_params=PARAMS,
    )(*args)
    return list(results)


def finish(args, shape, chunk, before=None):
    args = args + ([] if before is None else [before])
    return pl.pallas_call(
        partial(last_kernel, chunk),
        out_shape=shape,
        in_specs=[VM] * 4 + [HB] * (len(args) - 4),
        out_specs=HB,
        input_output_aliases={} if before is None else {4: 0},
        scratch_shapes=[pltpu.VMEM((2, *shape.shape[2:]), F32), pltpu.SemaphoreType.DMA((4,))],
        cost_estimate=cost([shape], args[:3], 0),
        compiler_params=PARAMS,
    )(*args)


def paired(state, unitaries, gate_order, gate_starts, pair):
    devices = lax.axis_size("qa")
    count = unitaries.shape[0] // 3
    gdim = unitaries.shape[-1]
    lanes, rows, dim, half = gdim, 4 * gdim, 2 * gdim, gdim
    f32 = partial(jax.ShapeDtypeStruct, dtype=F32)
    bf16 = partial(jax.ShapeDtypeStruct, dtype=BF16)
    tie = lax.optimization_barrier
    far = partial(pltpu.with_memory_space_constraint, memory_space=pltpu.HBM)
    _, h1 = my_bits()

    def other(v, bit):
        return lax.ppermute(v, "qa", [(i, i ^ bit) for i in range(devices)])

    def block_of(v, c):
        return lax.dynamic_slice_in_dim(v, (1 - h1) * 2 + c, 1, axis=0)

    view = state.reshape(2, -1, lanes).transpose(1, 0, 2).reshape(4, rows, lanes)
    came = [other(block_of(view, c), 2) for c in range(2)]
    step = 3 * 2 * (2 * gdim) * (2 * gdim) * (4 * gdim)
    enter_flops = 6 * rows * rows * lanes
    block, both = f32((1, rows, lanes)), f32((2, rows, lanes))
    m = f32((2, dim, gdim))
    m_scratch = pltpu.VMEM(m.shape, F32)
    small = [gate_order, gate_starts, pair]
    ngates = unitaries.shape[0]
    tile = (8, lanes)
    dma = pltpu.SemaphoreType.DMA
    w0, w1, units, flags, coef = call(
        front_kernel,
        [
            bf16((2, 3, dim, dim)),
            bf16((2, 2, half, rows)),
            f32((count, *unitaries.shape[1:])),
            jax.ShapeDtypeStruct(tile, jnp.int32),
            f32((2, 2, 2, *tile)),
        ],
        [far(v) for v in (*small, unitaries)],
        [HB] * 4,
        [pltpu.SMEM(v.shape, v.dtype) for v in small]
        + [pltpu.VMEM(unitaries.shape, F32), m_scratch, m_scratch]
        + [dma((3,)), dma((ngates,)), dma((count,))],
        flops=2 * count * step,
    )
    (kept,) = call(kept_kernel, [both], [w0, view], [VM] * 2, flops=2 * enter_flops)
    kept_other = other(kept, 1)
    units, kept = tie((units, kept))
    re2, im2 = call(half_kernel, [m, m], [units, flags], [VM] * 2, flops=count * step // 2)
    came[0], re2 = tie((came[0], re2))
    (mine,) = call(came_kernel, [block], [w0, came[0]], [VM] * 2, flops=enter_flops)
    re2, mine = tie((re2, mine))
    (w2,) = call(
        third_kernel,
        [bf16((2, 3, dim, dim))],
        [units, flags, re2, im2],
        [VM] * 4,
        [m_scratch, m_scratch],
        flops=count * step // 2,
    )

    def rest(c, mine):
        theirs = other(mine, 1)
        blocks = [w1, w2, kept, kept_other, mine, theirs]
        (back,) = call(partial(back_kernel, c), [block], blocks, [VM] * 6, flops=2 * enter_flops)
        return blocks, other(back, 2)

    def keep(c, blocks):
        return call(
            partial(keep_kernel, c),
            [block, block],
            [coef, *blocks],
            [VM] * 7,
            flops=2 * enter_flops,
        )

    shape = f32((2, 2, rows, lanes))
    blocks0, back0 = rest(0, mine)
    (mine,) = call(came_kernel, [block], [w0, came[1]], [VM] * 2, flops=enter_flops)
    blocks1, back1 = rest(1, mine)
    blocks0[0], blocks1[4] = tie((blocks0[0], blocks1[4]))
    keep0 = keep(0, blocks0)
    keep1 = keep(1, blocks1)
    back0, keep1[0] = tie((back0, keep1[0]))
    out = finish([*keep0, back0, coef], shape, 0)
    out = finish([*keep1, back1, coef], shape, 1, out)
    return out.reshape(-1, 2, lanes).transpose(1, 0, 2).reshape(2, -1)


def meets_two(state, unitaries, devices):
    local_bits = state.shape[1].bit_length() - 1
    global_bits = devices.bit_length() - 1
    top = 2 * (unitaries.shape[-1].bit_length() - 1) + 1
    met = top - (local_bits - global_bits)
    return met == 2 and local_bits == top + 2 and global_bits >= 2


def shards(*args):
    if meets_two(args[0], args[1], lax.axis_size("qa")):
        return paired(*args)
    return general(*args)


def solution(mesh):
    placed = (P(None, ("cuts", "qa")), P(), P(), P(), P())
    return jax.shard_map(
        shards, mesh=mesh, in_specs=placed, out_specs=P(None, ("cuts", "qa")), check_vma=False
    )
```

```python
from functools import partial

import jax
import jax.numpy as jnp
from jax import lax
from jax.experimental import pallas as pl
from jax.experimental.pallas import tpu as pltpu
from jax.sharding import PartitionSpec as P


HIGH = lax.Precision.HIGHEST
F32 = jnp.float32
BF16 = jnp.bfloat16


def mix(mat, vec):
    return jnp.einsum("ij,ajb->aib", mat, vec, precision=HIGH)


def dense_branch(re_part, im_part, u_re, u_im, offset):
    gdim = u_re.shape[0]
    gq = gdim.bit_length() - 1
    block = 2 ** (gq + offset)
    shaped_re = re_part.reshape(-1, gdim, block)
    shaped_im = im_part.reshape(-1, gdim, block)
    new_re = mix(u_re, shaped_re) - mix(u_im, shaped_im)
    new_im = mix(u_re, shaped_im) + mix(u_im, shaped_re)
    return (new_re.reshape(-1), new_im.reshape(-1))


def dense_gate(stacked, unitaries, gate_order, gate_starts, k):
    chosen = unitaries[gate_order[k]]
    branches = [partial(dense_branch, offset=0), partial(dense_branch, offset=1)]
    new_re, new_im = lax.switch(
        gate_starts[k], branches, stacked[0], stacked[1], chosen[0], chosen[1]
    )
    return jnp.stack([new_re, new_im])


def one_qubit(stacked, gate, qubit):
    shaped = stacked.reshape(2, -1, 2, 2**qubit)
    u_re, u_im = (gate[0], gate[1])
    new_re = jnp.einsum("bc,acx->abx", u_re, shaped[0], precision=HIGH) - jnp.einsum(
        "bc,acx->abx", u_im, shaped[1], precision=HIGH
    )
    new_im = jnp.einsum("bc,acx->abx", u_re, shaped[1], precision=HIGH) + jnp.einsum(
        "bc,acx->abx", u_im, shaped[0], precision=HIGH
    )
    return jnp.stack([new_re, new_im]).reshape(2, -1)


def swap_qubits(stacked):
    devices = lax.axis_size("qa")
    shaped = stacked.reshape(2, devices, -1)
    moved = lax.all_to_all(shaped, "qa", split_axis=1, concat_axis=1, tiled=True)
    return moved.reshape(2, -1)


def general(state, unitaries, gate_order, gate_starts, pair_gates):
    local_bits = state.shape[1].bit_length() - 1
    global_bits = lax.axis_size("qa").bit_length() - 1
    ngates = unitaries.shape[0]
    third = ngates // 3
    stacked = state
    for k in range(third):
        stacked = dense_gate(stacked, unitaries, gate_order, gate_starts, k)
    stacked = one_qubit(stacked, pair_gates[0], local_bits - 1)
    stacked = swap_qubits(stacked)
    for k in range(third, 2 * third):
        stacked = dense_gate(stacked, unitaries, gate_order, gate_starts, k)
    stacked = one_qubit(stacked, pair_gates[1], local_bits - global_bits)
    stacked = swap_qubits(stacked)
    for k in range(2 * third, ngates):
        stacked = dense_gate(stacked, unitaries, gate_order, gate_starts, k)
    return stacked


def split(x):
    hi = x.astype(BF16)
    return hi, (x - hi.astype(F32)).astype(BF16)


def dot3(w_hi, w_lo, x):
    x_hi, x_lo = split(x)
    return jnp.dot(
        jnp.concatenate([w_hi, w_hi, w_lo], axis=1),
        jnp.concatenate([x_hi, x_lo, x_hi], axis=0),
        preferred_element_type=F32,
    )


def dot_narrow(w_hi, w_lo, x):
    n = x.shape[1]
    beside = jnp.concatenate(split(x), axis=1)
    y = jnp.dot(
        jnp.concatenate([w_hi, w_lo], axis=1),
        jnp.concatenate([beside, beside], axis=0),
        preferred_element_type=F32,
    )
    return y[:, :n] + y[:, n:]


def embed(re, im):
    return jnp.concatenate(
        [jnp.concatenate([re, -im], axis=1), jnp.concatenate([im, re], axis=1)], axis=0
    )


def my_bits():
    me = lax.axis_index("qa")
    return lax.rem(me, 2), lax.rem(lax.div(me, 2), 2)


def halves(gdim, start):
    if start == 0:
        return [pl.ds(b * gdim, gdim) for b in range(2)]
    return [pl.ds(b, gdim, stride=2) for b in range(2)]


def begin(u_re, u_im, off, flip, m):
    gdim = u_re.shape[0]
    row = lax.broadcasted_iota(jnp.int32, (gdim, 2 * gdim), 0)
    col = jnp.bitwise_xor(lax.broadcasted_iota(jnp.int32, (gdim, 2 * gdim), 1), flip)
    ones = jnp.concatenate(
        [
            jnp.where(row * (1 + off) + b * (gdim - off * (gdim - 1)) == col, 1.0, 0.0)
            for b in range(2)
        ],
        axis=1,
    ).astype(BF16)
    w_hi, w_lo = split(jnp.concatenate([u_re, u_im], axis=0))
    y = jnp.dot(
        jnp.concatenate([w_hi, w_lo], axis=1),
        jnp.concatenate([ones, ones], axis=0),
        preferred_element_type=F32,
    )
    for start in range(2):

        @pl.when(off == start)
        def _():
            store(m, [(r, j) for r in halves(gdim, start) for j in range(2)], y)


def store(m, blocks, y):
    gdim = y.shape[0] // 2
    for i, (r, j) in enumerate(blocks):
        for p in range(2):
            m[p][j, r, :] = y[p * gdim : (p + 1) * gdim, gdim * i : gdim * (i + 1)]


def apply(u_re, u_im, off, source, m):
    gdim = u_re.shape[0]
    w_hi, w_lo = split(embed(u_re, u_im))
    for start in range(2):

        @pl.when(off == start)
        def _():
            blocks = [(r, j) for r in halves(gdim, start) for j in range(2)]
            x = jnp.concatenate(
                [jnp.concatenate([v[j, r, :] for v in source], axis=0) for r, j in blocks],
                axis=1,
            )
            store(m, blocks, dot3(w_hi, w_lo, x))


def compose(count, flip, gate, m):
    begin(*gate(0), flip, m)

    def step(i, carry):
        apply(*gate(i), m, m)
        return carry

    lax.fori_loop(1, count, step, 0)


def put(ref, re, im):
    for i, w in enumerate((re, im - re, -(re + im))):
        ref[0, i], ref[1, i] = split(w)


def times(w_ref, re, im, product):
    both, t_re, t_im = (
        product(w_ref[0, i], w_ref[1, i], x) for i, x in enumerate((re + im, re, im))
    )
    return both + t_im, both + t_re


def whole(m):
    return jnp.concatenate([m[j] for j in range(2)], axis=1)


def parts_of(ref, at):
    rows = ref.shape[1] // 2
    return ref[at, pl.ds(0, rows, stride=2), :], ref[at, pl.ds(1, rows, stride=2), :]


def front_kernel(order, starts, pair, unit, w0_ref, w1_ref, re, im, units, flags, coef, *scratch):
    order_s, starts_s, pair_s, u, m_re, m_im, small_sems, sems, late_sems = scratch
    ngates, later, gdim = unit.shape[0], units.shape[0], unit.shape[-1]
    count, half = ngates - later, gdim // 2
    h0, h1 = my_bits()
    smalls = [
        pltpu.make_async_copy(a, b, small_sems.at[i])
        for i, (a, b) in enumerate(((order, order_s), (starts, starts_s), (pair, pair_s)))
    ]
    for c in smalls:
        c.start()

    def fetch(g):
        return pltpu.make_async_copy(unit.at[g], u.at[g], sems.at[g])

    def late(k):
        return pltpu.make_async_copy(unit.at[order_s[count + k]], units.at[k], late_sems.at[k])

    for g in range(ngates):
        fetch(g).start()
    for c in smalls:
        c.wait()
    for k in range(later):
        late(k).start()

    def gate(i):
        g = order_s[i]
        fetch(g).wait()
        return u[g, 0], u[g, 1], starts_s[i]

    compose(later, 0, gate, (m_re, m_im))
    put(w0_ref, whole(m_re), whole(m_im))
    compose(later, h1 * gdim + h0 * half, lambda i: gate(later + i), (m_re, m_im))
    for k in range(2):
        at = lax.rem(h1 + k, 2) * gdim
        r, i = 0.0, 0.0
        for b in range(2):
            rows = pl.ds(pl.multiple_of(at + b * half, half), half)
            v_re, v_im = pair_s[1, 0, h0, b], pair_s[1, 1, h0, b]
            x_re, x_im = (
                jnp.concatenate([m[j, rows, :] for j in range(2)], axis=1) for m in (m_re, m_im)
            )
            r += v_re * x_re - v_im * x_im
            i += v_re * x_im + v_im * x_re
        w1_ref[0, k], w1_ref[1, k] = split(embed(r, i))
    late(0).wait()
    begin(units[0, 0], units[0, 1], starts_s[count], 0, (re, im))
    bits = starts_s[count]
    for k in range(1, later):
        bits += starts_s[count + k] * 2**k
    flags[...] = jnp.full(flags.shape, bits, jnp.int32)
    for b in range(2):
        for p in range(2):
            for i, v in enumerate((pair_s[0, p, b, h1], pair_s[0, p, b, 1 - h1])):
                coef[i, b, p] = jnp.full(coef.shape[3:], v, F32)
    for k in range(later):
        fetch(order_s[count + k]).wait()
        if k:
            late(k).wait()


def chosen(units, flags):
    bits = jnp.max(flags[...])

    def gate(k):
        return units[k, 0], units[k, 1], jnp.bitwise_and(lax.shift_right_logical(bits, k), 1)

    return gate


def half_kernel(units, flags, re1, im1, re, im):
    gate = chosen(units, flags)
    source = (re1, im1)
    for k in range(1, units.shape[0] // 2):
        apply(*gate(k), source, (re, im))
        source = (re, im)


def third_kernel(units, flags, re, im, w_ref, m_re, m_im):
    count = units.shape[0]
    gate = chosen(units, flags)
    source = (re, im)
    for k in range(count // 2, count):
        apply(*gate(k), source, (m_re, m_im))
        source = (m_re, m_im)
    put(w_ref, whole(source[0]), whole(source[1]))


def kept_kernel(w_ref, state, out):
    _, h1 = my_bits()
    rows, lanes = state.shape[1] // 2, state.shape[2]
    blocks = [parts_of(state, h1 * 2 + c) for c in range(2)]
    y = times(w_ref, *(jnp.concatenate(v, axis=1) for v in zip(*blocks)), dot3)
    for k in range(2):
        for p in range(2):
            out[k, p * rows : (p + 1) * rows] = y[p][:, k * lanes : (k + 1) * lanes]


def came_kernel(w_ref, raw, out):
    rows = raw.shape[1] // 2
    out[0, :rows], out[0, rows:] = times(w_ref, *parts_of(raw, 0), dot_narrow)


def through(k, chunk, w1_ref, w2_ref, kept, kept_other, mine, theirs):
    lanes = mine.shape[2]
    dim = mine.shape[1] // 2
    part = dim // 4
    sources = ((kept, chunk), (kept_other, chunk), (mine, 0), (theirs, 0))
    cols = [
        jnp.concatenate(
            [v[i, p * dim + f * part : p * dim + (f + 1) * part, :] for p in range(2) for v, i in sources],
            axis=0,
        )
        for f in range(4)
    ]
    y = dot3(w1_ref[0, k], w1_ref[1, k], jnp.concatenate(cols, axis=1))
    x = (
        jnp.concatenate(
            [y[p * part : (p + 1) * part, f * lanes : (f + 1) * lanes] for f in range(4)], axis=0
        )
        for p in range(2)
    )
    return times(w2_ref, *x, dot_narrow)


def back_kernel(chunk, *refs):
    out = refs[-1]
    dim = out.shape[1] // 2
    out[0, :dim], out[0, dim:] = through(1, chunk, *refs[:-1])


def keep_kernel(chunk, coef, *refs):
    k_re, k_im = through(0, chunk, *refs[:-2])
    dim = k_re.shape[0]
    for b, out in enumerate(refs[-2:]):
        v_re, v_im = coef[0, b, 0][:1], coef[0, b, 1][:1]
        out[0, :dim, :] = v_re * k_re - v_im * k_im
        out[0, dim:, :] = v_re * k_im + v_im * k_re


def last_kernel(chunk, part0, part1, back, coef, *refs):
    out, buf, sems = refs[-3:]
    rows = back.shape[1] // 2
    cut = rows // 2
    copies = []
    for b, part in enumerate((part0, part1)):
        for q in range(2):
            at = q * cut
            u_re, u_im = coef[1, b, 0][:1], coef[1, b, 1][:1]
            re, im = pl.ds(at, cut), pl.ds(rows + at, cut)
            b_re, b_im = back[0, re, :], back[0, im, :]
            buf[b, pl.ds(2 * at, cut, stride=2), :] = part[0, re, :] + (u_re * b_re - u_im * b_im)
            buf[b, pl.ds(2 * at + 1, cut, stride=2), :] = part[0, im, :] + (u_re * b_im + u_im * b_re)
            span = pl.ds(2 * at, 2 * cut)
            copies.append(
                pltpu.make_async_copy(
                    buf.at[b, span], out.at[b, chunk, span], sems.at[2 * b + q]
                )
            )
            copies[-1].start()
    for c in copies:
        c.wait()


VM = pl.BlockSpec(memory_space=pltpu.VMEM)
SM = pl.BlockSpec(memory_space=pltpu.SMEM)
HB = pl.BlockSpec(memory_space=pltpu.HBM)


def cost(outs, args, flops):
    nbytes = sum(a.size * a.dtype.itemsize for a in (*outs, *args))
    return pl.CostEstimate(flops=flops, bytes_accessed=nbytes, transcendentals=0)


PARAMS = pltpu.CompilerParams(vmem_limit_bytes=16 * 2**20)


def call(body, outs, args, specs, scratch=(), flops=0):
    results = pl.pallas_call(
        body,
        out_shape=outs,
        in_specs=specs,
        out_specs=[VM] * len(outs),
        scratch_shapes=scratch,
        cost_estimate=cost(outs, args, flops),
        compiler_params=PARAMS,
    )(*args)
    return list(results)


def finish(args, shape, chunk, before=None):
    args = args + ([] if before is None else [before])
    return pl.pallas_call(
        partial(last_kernel, chunk),
        out_shape=shape,
        in_specs=[VM] * 4 + [HB] * (len(args) - 4),
        out_specs=HB,
        input_output_aliases={} if before is None else {4: 0},
        scratch_shapes=[pltpu.VMEM((2, *shape.shape[2:]), F32), pltpu.SemaphoreType.DMA((4,))],
        cost_estimate=cost([shape], args[:3], 0),
        compiler_params=PARAMS,
    )(*args)


def paired(state, unitaries, gate_order, gate_starts, pair):
    devices = lax.axis_size("qa")
    count = unitaries.shape[0] // 3
    gdim = unitaries.shape[-1]
    lanes, rows, dim, half = gdim, 4 * gdim, 2 * gdim, gdim
    f32 = partial(jax.ShapeDtypeStruct, dtype=F32)
    bf16 = partial(jax.ShapeDtypeStruct, dtype=BF16)
    tie = lax.optimization_barrier
    far = partial(pltpu.with_memory_space_constraint, memory_space=pltpu.HBM)
    _, h1 = my_bits()

    def other(v, bit):
        return lax.ppermute(v, "qa", [(i, i ^ bit) for i in range(devices)])

    def block_of(v, c):
        return lax.dynamic_slice_in_dim(v, (1 - h1) * 2 + c, 1, axis=0)

    view = state.reshape(2, -1, lanes).transpose(1, 0, 2).reshape(4, rows, lanes)
    came = [other(block_of(view, c), 2) for c in range(2)]
    step = 3 * 2 * (2 * gdim) * (2 * gdim) * (4 * gdim)
    enter_flops = 6 * rows * rows * lanes
    block, both = f32((1, rows, lanes)), f32((2, rows, lanes))
    m = f32((2, dim, gdim))
    m_scratch = pltpu.VMEM(m.shape, F32)
    small = [gate_order, gate_starts, pair]
    ngates = unitaries.shape[0]
    tile = (8, lanes)
    dma = pltpu.SemaphoreType.DMA
    w0, w1, re1, im1, units, flags, coef = call(
        front_kernel,
        [
            bf16((2, 3, dim, dim)),
            bf16((2, 2, half, rows)),
            m,
            m,
            f32((count, *unitaries.shape[1:])),
            jax.ShapeDtypeStruct(tile, jnp.int32),
            f32((2, 2, 2, *tile)),
        ],
        [far(v) for v in (*small, unitaries)],
        [HB] * 4,
        [pltpu.SMEM(v.shape, v.dtype) for v in small]
        + [pltpu.VMEM(unitaries.shape, F32), m_scratch, m_scratch]
        + [dma((3,)), dma((ngates,)), dma((count,))],
        flops=2 * count * step,
    )
    (kept,) = call(kept_kernel, [both], [w0, view], [VM] * 2, flops=2 * enter_flops)
    kept_other = other(kept, 1)
    units, kept = tie((units, kept))
    re2, im2 = call(half_kernel, [m, m], [units, flags, re1, im1], [VM] * 4, flops=step)
    came[0], re2 = tie((came[0], re2))
    (mine,) = call(came_kernel, [block], [w0, came[0]], [VM] * 2, flops=enter_flops)
    re2, mine = tie((re2, mine))
    (w2,) = call(
        third_kernel,
        [bf16((2, 3, dim, dim))],
        [units, flags, re2, im2],
        [VM] * 4,
        [m_scratch, m_scratch],
        flops=count * step // 2,
    )

    def rest(c, mine):
        theirs = other(mine, 1)
        blocks = [w1, w2, kept, kept_other, mine, theirs]
        (back,) = call(partial(back_kernel, c), [block], blocks, [VM] * 6, flops=2 * enter_flops)
        return blocks, other(back, 2)

    def keep(c, blocks):
        return call(
            partial(keep_kernel, c),
            [block, block],
            [coef, *blocks],
            [VM] * 7,
            flops=2 * enter_flops,
        )

    shape = f32((2, 2, rows, lanes))
    blocks0, back0 = rest(0, mine)
    (mine,) = call(came_kernel, [block], [w0, came[1]], [VM] * 2, flops=enter_flops)
    blocks1, back1 = rest(1, mine)
    blocks0[0], blocks1[4] = tie((blocks0[0], blocks1[4]))
    keep0 = keep(0, blocks0)
    keep1 = keep(1, blocks1)
    back0, keep1[0] = tie((back0, keep1[0]))
    out = finish([*keep0, back0, coef], shape, 0)
    out = finish([*keep1, back1, coef], shape, 1, out)
    return out.reshape(-1, 2, lanes).transpose(1, 0, 2).reshape(2, -1)


def meets_two(state, unitaries, devices):
    local_bits = state.shape[1].bit_length() - 1
    global_bits = devices.bit_length() - 1
    top = 2 * (unitaries.shape[-1].bit_length() - 1) + 1
    met = top - (local_bits - global_bits)
    return met == 2 and local_bits == top + 2 and global_bits >= 2


def shards(*args):
    if meets_two(args[0], args[1], lax.axis_size("qa")):
        return paired(*args)
    return general(*args)


def solution(mesh):
    placed = (P(None, ("cuts", "qa")), P(), P(), P(), P())
    return jax.shard_map(
        shards, mesh=mesh, in_specs=placed, out_specs=P(None, ("cuts", "qa")), check_vma=False
    )
```
